32 devices in a mesh: side: 2 (over y), gx: 4 (over x, core), gy: 4 (over z).
Axes of the slice: x: 2, y: 2, z: 4, core: 2. Of those that a mesh axis runs over, the one named last changes fastest.
Arguments:
- populations: float32 [2, 19, 4, 128, 512], P('side', None, None, 'gx', 'gy'), may hold values from 0.01 to 0.84, as said below
- solid_mask: int32 [2, 4, 128, 512], P('side', None, 'gx', 'gy'), may hold values 0 or 1
- water_sheet: float32 [32, 128, 512], P(None, 'gx', ('side', 'gy')), may hold values from 2 to 12
- current: float32 [128, 512], P('gx', ('side', 'gy')), may hold values from 0.5 to 3
Outputs:
- populations_out: float32 [2, 19, 4, 128, 512], P('side', None, None, 'gx', 'gy')
- sheet_out: float32 [32, 128, 512], P(None, 'gx', ('side', 'gy'))
The draws below stay inside these ranges and needn't reach their ends.
Inputs may be any that keep to these rules, and one draw needn't show every extreme that they name: `populations`: every population is positive.
All inputs are finite; a program needn't handle non-finite values. No bound on the sum of `solid_mask` on one device may be relied on, other than what follows from the above.
Results may differ from the reference program's by a relative error of at most 0.0003.
Values sent between devices are 32-bit elements; how exact they have to be, the bound alone decides.
No kernel may reach another device: no remote copies, remote signals or barrier semaphores. Data moves between devices by JAX's collectives and lax.ppermute only.
A program may use at most 64 MiB of HBM per device.

```python
import jax
import jax.numpy as jnp

LAYERS = 4
MEMBRANE = 32
STEPS = 8
SUBSTEPS = 2
NX = 128
NY = 512
N_GY = 4


def draw_populations(key, part):
    weights = jnp.array((1.0 / 3.0,) + (1.0 / 18.0,) * 6 + (1.0 / 36.0,) * 12, jnp.float32)
    density_key = jax.random.fold_in(key, 11)
    noise_key = jax.random.fold_in(key, 23)
    log_density = jax.random.uniform(density_key, (2, 1, LAYERS, NX, NY), jnp.float32, jnp.log(0.5), jnp.log(2.0))
    noise = 0.2 * jax.random.uniform(noise_key, (2, 19, LAYERS, NX, NY), jnp.float32, -1.0, 1.0)
    return weights[None, :, None, None, None] * jnp.exp(log_density) * (1.0 + noise)


def with_ends(values, key, least, largest):
    longest = values.shape.index(max(values.shape))
    spots = []
    for shift in (0, 1):
        where = [jax.random.randint(jax.random.fold_in(key, axis), (), 0, length) for axis, length in enumerate(values.shape)]
        where[longest] = (where[longest] + shift) % values.shape[longest]
        spots.append(tuple(where))
    return values.at[spots[0]].set(least).at[spots[1]].set(largest)


def level_of(own_key, dims, pieces, low, high):
    def one(axis_at, shards_of):
        heights = jax.random.uniform(jax.random.fold_in(jax.random.fold_in(own_key, 6), axis_at), (shards_of,), jnp.float32, low / len(pieces), high / len(pieces))
        return jnp.repeat(jnp.exp(heights), dims[axis_at] // shards_of).reshape((-1,) + (1,) * (len(dims) - axis_at - 1))

    loudness = one(*pieces[0])
    for cut in pieces[1:]:
        loudness = loudness * one(*cut)
    return loudness


def setup_inputs(seed: int = 0) -> dict:
    splits = jax.random.split(jax.random.key(seed), 5)
    return {
        "populations": draw_populations(jax.random.fold_in(splits[4], 71), 0),
        "solid_mask": with_ends((jax.random.randint(splits[1], (2, LAYERS, NX, NY), 0, 4) < 3).astype(jnp.int32), jax.random.fold_in(splits[1], 1), 0, 1),
        "water_sheet": jnp.clip(2.0 + 10.0 * jax.random.uniform(splits[2], (MEMBRANE, NX, NY), jnp.float32) ** level_of(splits[2], (MEMBRANE, NX, NY), ((1, 4), (2, 8)), -0.2, 0.2), 2.0, 12.0),
        "current": jnp.clip(0.5 + 2.5 * jax.random.uniform(splits[3], (NX, NY), jnp.float32) ** level_of(splits[3], (NX, NY), ((0, 4), (1, 8)), -0.2, 0.2), 0.5, 3.0),
    }


velocity_table = ((0, 0, 0), (1, 0, 0), (-1, 0, 0), (0, 1, 0), (0, -1, 0), (0, 0, 1), (0, 0, -1),
                  (1, 1, 0), (-1, -1, 0), (1, -1, 0), (-1, 1, 0), (1, 0, 1), (-1, 0, -1),
                  (1, 0, -1), (-1, 0, 1), (0, 1, 1), (0, -1, -1), (0, 1, -1), (0, -1, 1))
opposite_index = (0, 2, 1, 4, 3, 6, 5, 8, 7, 10, 9, 12, 11, 14, 13, 16, 15, 18, 17)
weight_table = (1.0 / 3.0,) + (1.0 / 18.0,) * 6 + (1.0 / 36.0,) * 12
relax_time = 0.8
coupling = -3.0
wall_potential = 0.4
uptake_rate = 0.02
drag_rate = 0.03
base_diffusion = 0.05
slope_diffusion = 0.015


def density(fields):
    summed = fields[0]
    for direction in range(1, 19):
        summed = summed + fields[direction]
    return summed


def potential(density_now, solids):
    return jnp.where(solids > 0, 1.0 - jnp.exp(-density_now), wall_potential)


def attraction(padded):
    layers = padded.shape[0]
    inner_rows = padded.shape[1] - 2
    inner_cols = padded.shape[2] - 2
    zeros_layer = jnp.zeros((1,) + padded.shape[1:], jnp.float32)
    stacked = jnp.concatenate([zeros_layer, padded, zeros_layer], axis=0)
    totals = [None, None, None]
    for direction in range(1, 19):
        shift_x, shift_y, shift_z = velocity_table[direction]
        weighted = weight_table[direction] * stacked[1 + shift_z:1 + shift_z + layers,
                                                     1 + shift_x:1 + shift_x + inner_rows,
                                                     1 + shift_y:1 + shift_y + inner_cols]
        for component in range(3):
            factor = velocity_table[direction][component]
            if factor != 0:
                contribution = factor * weighted
                totals[component] = contribution if totals[component] is None else totals[component] + contribution
    centre = padded[:, 1:-1, 1:-1]
    return [-coupling * centre * summed for summed in totals]


def relax(fields, density_now, solids, padded):
    forces = attraction(padded)
    velocity = []
    for component in range(3):
        moment = None
        for direction in range(1, 19):
            factor = velocity_table[direction][component]
            if factor != 0:
                contribution = factor * fields[direction]
                moment = contribution if moment is None else moment + contribution
        velocity.append((moment + relax_time * forces[component]) / density_now)
    speed_squared = velocity[0] * velocity[0] + velocity[1] * velocity[1] + velocity[2] * velocity[2]
    is_pore = solids > 0
    relaxed = []
    for direction in range(19):
        projected = jnp.zeros_like(density_now)
        for component in range(3):
            factor = velocity_table[direction][component]
            if factor != 0:
                projected = projected + factor * velocity[component]
        balance = weight_table[direction] * density_now * (
            1.0 + 3.0 * projected + 4.5 * projected * projected - 1.5 * speed_squared)
        collided = fields[direction] - (fields[direction] - balance) / relax_time
        relaxed.append(jnp.where(is_pore, collided, fields[opposite_index[direction]]))
    return jnp.stack(relaxed)


def propagate(padded, membrane_flux):
    inner_rows = padded.shape[2] - 2
    inner_cols = padded.shape[3] - 2
    centre = padded[:, :, 1:-1, 1:-1]
    result = []
    for direction in range(19):
        shift_x, shift_y, shift_z = velocity_table[direction]
        moved = padded[direction, :, 1 - shift_x:1 - shift_x + inner_rows, 1 - shift_y:1 - shift_y + inner_cols]
        if shift_z == 1:
            inflow = centre[opposite_index[direction], :1] - 6.0 * weight_table[direction] * membrane_flux[None]
            moved = jnp.concatenate([inflow, moved[:-1]], axis=0)
        elif shift_z == -1:
            moved = jnp.concatenate([moved[1:], centre[opposite_index[direction], -1:]], axis=0)
        result.append(moved)
    return jnp.stack(result)


def uptake(density_row):
    activity = density_row / (1.0 + density_row)
    return 0.043 + activity * (17.18 + activity * (-39.85 + 36.0 * activity))


def sheet_substep(water, current_rows, inflow_anode, inflow_cathode):
    diffusivity = base_diffusion + slope_diffusion * water
    face_z = -0.5 * (diffusivity[1:] + diffusivity[:-1]) * (water[1:] - water[:-1]) + drag_rate * current_rows[None] * water[:-1]
    change = jnp.concatenate([inflow_anode[None], face_z]) - jnp.concatenate([face_z, -inflow_cathode[None]])
    return water + change


def reference(populations, solid_mask, water_sheet, current):
    groups = 2 * N_GY
    sub_width = NY // (groups * N_GY)

    def to_sheet(field):
        return field.reshape(NX, N_GY, groups, sub_width).transpose(0, 2, 1, 3).reshape(NX, NY)

    def from_sheet(field):
        return field.reshape(NX, groups, N_GY, sub_width).transpose(0, 2, 1, 3).reshape(NX, NY)

    surface_anode = to_sheet(density(populations[0][:, :1])[0])
    surface_cathode = to_sheet(density(populations[1][:, :1])[0])
    inflow_anode = uptake_rate * (uptake(surface_anode) - water_sheet[0])
    inflow_cathode = uptake_rate * (uptake(surface_cathode) - water_sheet[-1])
    water = water_sheet
    for repeat in range(SUBSTEPS):
        water = sheet_substep(water, current, inflow_anode, inflow_cathode)
    results = []
    for which_side, inflow in ((0, inflow_anode), (1, inflow_cathode)):
        membrane_flux = from_sheet(inflow)
        lattice = populations[which_side]
        solids = solid_mask[which_side]
        for repeat in range(STEPS):
            density_now = density(lattice)
            padded = jnp.pad(potential(density_now, solids), ((0, 0), (1, 1), (1, 1)), mode="wrap")
            relaxed = relax(lattice, density_now, solids, padded)
            lattice = propagate(jnp.pad(relaxed, ((0, 0), (0, 0), (1, 1), (1, 1)), mode="wrap"), membrane_flux)
        results.append(lattice)
    return jnp.stack(results), water
```

```python
import functools

import jax
import jax.numpy as jnp
from jax import lax
from jax.experimental import pallas as pl
from jax.experimental.pallas import tpu as pltpu
from jax.sharding import PartitionSpec as P

STEPS = 8
SUBSTEPS = 2
HALO = 2 * STEPS
TILE = 8
LANES = 128

velocity_table = (
    (0, 0, 0),
    (1, 0, 0),
    (-1, 0, 0),
    (0, 1, 0),
    (0, -1, 0),
    (0, 0, 1),
    (0, 0, -1),
    (1, 1, 0),
    (-1, -1, 0),
    (1, -1, 0),
    (-1, 1, 0),
    (1, 0, 1),
    (-1, 0, -1),
    (1, 0, -1),
    (-1, 0, 1),
    (0, 1, 1),
    (0, -1, -1),
    (0, 1, -1),
    (0, -1, 1),
)
DIRS = len(velocity_table)
wall_potential = 0.4
uptake_rate = 0.02
drag_rate = 0.03
base_diffusion = 0.05
slope_diffusion = 0.015
ROOT2 = 2.0**0.5

VMEM = pl.BlockSpec(memory_space=pltpu.VMEM)


def uptake(density_row):
    activity = density_row / (1.0 + density_row)
    return 0.043 + activity * (17.18 + activity * (-39.85 + 36.0 * activity))


def spin(tile, shift):
    shift = shift % LANES
    return tile if shift == 0 else pltpu.roll(tile, shift, 1)


def lane_index():
    return lax.broadcasted_iota(jnp.int32, (TILE, LANES), 1)


def run_steps(fields, density_ref, psi_ref, pore_ref, flux_ref, layers, window_rows):
    def step_body(step, carry):
        here = lax.rem(step, 2)
        there = 1 - here
        first = 2 * step

        def potentials(tile, inner):
            row = first + TILE * tile
            rows = pl.ds(row, TILE)
            for z in range(layers):
                parts = [fields[here, i, z, rows, :] for i in range(DIRS)]
                while len(parts) > 1:
                    parts = [a + b for a, b in zip(parts[::2], parts[1::2])] + (
                        [parts[-1]] if len(parts) % 2 else []
                    )
                rho = parts[0]
                density_ref[z, rows, :] = rho
                psi_ref[z, rows, :] = jnp.where(
                    pore_ref[z, rows, :] > 0.5, 1.0 - jnp.exp(-rho), wall_potential
                )
            return inner

        lax.fori_loop(0, (window_rows - 2 * first + TILE - 1) // TILE, potentials, 0)

        def collide(tile, inner):
            row = first + 1 + TILE * tile
            rows = pl.ds(row, TILE)
            up = pl.ds(row + 1, TILE)
            down = pl.ds(row - 1, TILE)
            centre = [psi_ref[z, rows, :] for z in range(layers)]
            plus = [psi_ref[z, up, :] for z in range(layers)]
            minus = [psi_ref[z, down, :] for z in range(layers)]
            slope = [a - b for a, b in zip(plus, minus)]
            pair = [a + b for a, b in zip(plus, minus)]

            def across(values, z, sign):
                above = values[z + 1] if z + 1 < layers else None
                below = values[z - 1] if z > 0 else None
                if above is None and below is None:
                    return jnp.zeros((TILE, LANES), jnp.float32)
                if above is None:
                    return below if sign > 0 else -below
                if below is None:
                    return above
                return above + below if sign > 0 else above - below

            for z in range(layers):
                pull_x = (
                    (slope[z] + slope[z])
                    + across(slope, z, 1)
                    + (spin(slope[z], 1) + spin(slope[z], -1))
                )
                lift = across(centre, z, -1)
                pull_z = (lift + lift) + across(pair, z, -1) + (spin(lift, 1) + spin(lift, -1))
                shell = (centre[z] + centre[z]) + pair[z] + across(centre, z, 1)
                pull_y = spin(shell, -1) - spin(shell, 1)

                rho = density_ref[z, rows, :]
                is_pore = pore_ref[z, rows, :] > 0.5
                f = [fields[here, i, z, rows, :] for i in range(DIRS)]
                total = [None] + [f[i] + f[i + 1] for i in range(1, DIRS, 2)]
                delta = [None] + [f[i] - f[i + 1] for i in range(1, DIRS, 2)]
                moment = []
                for component in range(3):
                    terms = []
                    for k in range(1, 10):
                        factor = velocity_table[2 * k - 1][component]
                        if factor:
                            terms.append((factor, delta[k]))
                    value = terms[0][1]
                    for factor, term in terms[1:]:
                        value = value + term if factor > 0 else value - term
                    moment.append(value)
                pulled = centre[z] * (1.0 / 15.0)
                scale = jnp.where(is_pore, (3.0 / ROOT2) / rho, 0.0)
                u = [
                    (moment[c] + pulled * pull) * scale
                    for c, pull in enumerate((pull_x, pull_y, pull_z))
                ]
                base = 1.0 - (u[0] * u[0] + u[1] * u[1] + u[2] * u[2]) * (1.0 / 3.0)
                a_diag = jnp.where(is_pore, rho * (1.25 / 36.0), 0.0)
                a_axis = a_diag + a_diag
                o_diag = a_diag * ROOT2
                o_axis = a_axis * ROOT2
                keep_even = jnp.where(is_pore, -0.125, 0.5)
                keep_odd = jnp.where(is_pore, -0.125, -0.5)
                fields[there, 0, z, rows, :] = f[0] * (keep_even + keep_even) + base * (
                    a_diag * 12.0
                )
                for k in range(1, 10):
                    i = 2 * k - 1
                    e = velocity_table[i]
                    along = None
                    for component in range(3):
                        if e[component] == 0:
                            continue
                        if along is None:
                            along = u[component]
                        elif e[component] > 0:
                            along = along + u[component]
                        else:
                            along = along - u[component]
                    axis = k <= 3
                    even = total[k] * keep_even + (along * along + base) * (
                        a_axis if axis else a_diag
                    )
                    odd = delta[k] * keep_odd + along * (o_axis if axis else o_diag)
                    for j, sign, post in ((i, 1, even + odd), (i + 1, -1, even - odd)):
                        other = i + 1 if j == i else i
                        shift_x, shift_y, shift_z = (sign * v for v in e)
                        if z + shift_z < 0:
                            inflow = flux_ref[rows, :] * (1.0 / 3.0 if axis else 1.0 / 6.0)
                            fields[there, other, z, rows, :] = post - inflow
                        elif z + shift_z >= layers:
                            fields[there, other, z, rows, :] = post
                        else:
                            fields[there, j, z + shift_z, pl.ds(row + shift_x, TILE), :] = spin(
                                post, shift_y
                            )
            return inner

        lax.fori_loop(0, (window_rows - 2 - 2 * first + TILE - 1) // TILE, collide, 0)
        return carry

    lax.fori_loop(0, STEPS, step_body, 0)


def set_flux(fields, water_of, flux_ref, window_rows):
    def flux_rows(tile, carry):
        rows = pl.ds(TILE * tile, TILE)
        rho = fields[0, 0, 0, rows, :]
        for i in range(1, DIRS):
            rho = rho + fields[0, i, 0, rows, :]
        flux_ref[rows, :] = uptake_rate * (uptake(rho) - flux_ref[rows, :])
        return carry

    lax.fori_loop(0, window_rows // TILE, flux_rows, 0)


def middle_kernel(f_ref, mask_ref, water_ref, low_ref, high_ref, clow_ref, chigh_ref, out_ref,
                  fields, density_ref, psi_ref, pore_ref, flux_ref):
    layers, height = f_ref.shape[1], f_ref.shape[2]
    centre = slice(HALO, HALO + height)
    after = slice(HALO + height, 2 * HALO + height)

    def load(i, carry):
        for z in range(layers):
            fields[0, i, z, :HALO, :] = low_ref[i, z]
            fields[0, i, z, centre, :] = f_ref[i, z]
            fields[0, i, z, after, :] = high_ref[i, z]
        return carry

    lax.fori_loop(0, DIRS, load, 0)
    for z in range(layers):
        pore_ref[z, :HALO, :] = low_ref[DIRS, z]
        pore_ref[z, centre, :] = mask_ref[z].astype(jnp.float32)
        pore_ref[z, after, :] = high_ref[DIRS, z]
    flux_ref[:HALO, :] = clow_ref[DIRS + 1]
    flux_ref[centre, :] = water_ref[0]
    flux_ref[after, :] = chigh_ref[DIRS + 1]
    window_rows = height + 2 * HALO
    set_flux(fields, None, flux_ref, window_rows)
    run_steps(fields, density_ref, psi_ref, pore_ref, flux_ref, layers, window_rows)

    def save(i, carry):
        for z in range(layers):
            out_ref[i, z] = fields[STEPS % 2, i, z, centre, :]
        return carry

    lax.fori_loop(0, DIRS, save, 0)


def edge_kernel(f_ref, mask_ref, water_ref, low_ref, high_ref, left_ref, right_ref, clow_ref,
                chigh_ref, middle_ref, out_ref, fields, density_ref, psi_ref, pore_ref, flux_ref):
    layers, height = f_ref.shape[1], f_ref.shape[2]
    lane = lane_index()
    two = 2 * HALO
    low_tiles = HALO // TILE
    mid_tiles = height // TILE
    half_tiles = mid_tiles // 2
    half_lanes = LANES // 2
    right_at, left_at = two, LANES - 3 * HALO

    def join(own, left, right):
        outer = jnp.where(lane < two, spin(own, two), spin(own, -two))
        halo = jnp.where(lane < half_lanes, right, left)
        return jnp.where((lane < two) | (lane >= LANES - two), outer, halo)

    def own_tile(i, z, tile, kind):
        if tile < low_tiles:
            return low_ref[i, z, TILE * tile : TILE * (tile + 1), :]
        if tile < low_tiles + mid_tiles:
            t = tile - low_tiles
            if kind == "mask":
                return mask_ref[z, TILE * t : TILE * (t + 1), :].astype(jnp.float32)
            return f_ref[i, z, TILE * t : TILE * (t + 1), :]
        t = tile - low_tiles - mid_tiles
        return high_ref[i, z, TILE * t : TILE * (t + 1), :]

    def halo_tiles(i, z, tile):
        if low_tiles <= tile < low_tiles + mid_tiles:
            t = tile - low_tiles
            at = half_lanes * (t // half_tiles) + HALO * z
            rows = slice(TILE * (t % half_tiles), TILE * (t % half_tiles) + TILE)
            return (
                spin(left_ref[i, rows, :], left_at - at),
                spin(right_ref[i, rows, :], right_at - at),
            )
        ref = clow_ref if tile < low_tiles else chigh_ref
        t = tile if tile < low_tiles else tile - low_tiles - mid_tiles
        both = ref[i, TILE * t : TILE * (t + 1), :]
        return spin(both, left_at - HALO * z), spin(both, right_at - half_lanes - HALO * z)

    tiles = 2 * low_tiles + mid_tiles

    def load(i, carry):
        for z in range(layers):
            for tile in range(tiles):
                rows = slice(TILE * tile, TILE * (tile + 1))
                fields[0, i, z, rows, :] = join(own_tile(i, z, tile, "f"), *halo_tiles(i, z, tile))
        return carry

    lax.fori_loop(0, DIRS, load, 0)
    for z in range(layers):
        for tile in range(tiles):
            rows = slice(TILE * tile, TILE * (tile + 1))
            pore_ref[z, rows, :] = join(
                own_tile(DIRS, z, tile, "mask"), *halo_tiles(DIRS, z, tile)
            )
    for tile in range(tiles):
        rows = slice(TILE * tile, TILE * (tile + 1))
        if tile < low_tiles:
            own, extra = (clow_ref[DIRS + 1 + k, rows, :] for k in range(2))
        elif tile < low_tiles + mid_tiles:
            t = tile - low_tiles
            own, extra = (water_ref[k, TILE * t : TILE * (t + 1), :] for k in range(2))
        else:
            t = tile - low_tiles - mid_tiles
            own, extra = (chigh_ref[DIRS + 1 + k, TILE * t : TILE * (t + 1), :] for k in range(2))
        flux_ref[rows, :] = join(own, spin(extra, -two), spin(extra, two))
    window_rows = height + 2 * HALO
    set_flux(fields, None, flux_ref, window_rows)
    run_steps(fields, density_ref, psi_ref, pore_ref, flux_ref, layers, window_rows)

    def save(i, carry):
        for z in range(layers):
            for t in range(mid_tiles):
                rows = slice(TILE * t, TILE * (t + 1))
                edge = fields[STEPS % 2, i, z, HALO + TILE * t : HALO + TILE * (t + 1), :]
                edge = jnp.where(lane < half_lanes, spin(edge, two), spin(edge, -two))
                inside = (lane >= HALO) & (lane < LANES - HALO)
                out_ref[i, z, rows, :] = jnp.where(inside, middle_ref[i, z, rows, :], edge)
        return carry

    lax.fori_loop(0, DIRS, save, 0)


def window_scratch(layers, rows):
    padded = rows + TILE
    return [
        pltpu.VMEM((2, DIRS, layers, padded, LANES), jnp.float32),
        pltpu.VMEM((layers, padded, LANES), jnp.float32),
        pltpu.VMEM((layers, padded, LANES), jnp.float32),
        pltpu.VMEM((layers, padded, LANES), jnp.float32),
        pltpu.VMEM((padded, LANES), jnp.float32),
    ]


def strip_kernel(f_ref, mask_ref, left_ref, right_ref):
    layers, height = f_ref.shape[1], f_ref.shape[2]
    lane = lane_index()
    half_rows = height // 2
    half_lanes = LANES // 2

    def pack(i, read):
        for t in range(half_rows // TILE):
            rows = slice(TILE * t, TILE * (t + 1))
            first = last = None
            for h in range(2):
                for z in range(layers):
                    tile = read(z, slice(half_rows * h + TILE * t, half_rows * h + TILE * (t + 1)))
                    at = half_lanes * h + HALO * z
                    one = spin(tile, at)
                    two = spin(tile, at + HALO)
                    mine = lane >= at
                    first = one if first is None else jnp.where(mine, one, first)
                    last = two if last is None else jnp.where(mine, two, last)
            left_ref[i, rows, :] = first
            right_ref[i, rows, :] = last

    def each(i, carry):
        pack(i, lambda z, rows: f_ref[i, z, rows, :])
        return carry

    lax.fori_loop(0, DIRS, each, 0)
    pack(DIRS, lambda z, rows: mask_ref[z, rows, :].astype(jnp.float32))


def corner_kernel(left_ref, right_ref, water_ref, up_ref, down_ref):
    half_lanes = LANES // 2
    lane = lane_index()
    tiles = left_ref.shape[1] // TILE

    def each(i, carry):
        for t in range(tiles):
            rows = slice(TILE * t, TILE * (t + 1))
            left, right = left_ref[i, rows, :], right_ref[i, rows, :]
            up_ref[i, rows, :] = jnp.where(lane < half_lanes, spin(left, half_lanes), right)
            down_ref[i, rows, :] = jnp.where(lane < half_lanes, left, spin(right, half_lanes))
        return carry

    lax.fori_loop(0, DIRS + 1, each, 0)
    height = water_ref.shape[1]
    for k in range(2):
        up_ref[DIRS + 1 + k] = water_ref[k, height - HALO :, :]
        down_ref[DIRS + 1 + k] = water_ref[k, :HALO, :]


def whole_call(kernel, outs, scratch, flops, bytes_accessed):
    return pl.pallas_call(
        kernel,
        out_shape=outs,
        in_specs=None,
        out_specs=jax.tree.map(lambda _: VMEM, outs),
        scratch_shapes=scratch,
        cost_estimate=pl.CostEstimate(
            flops=flops, bytes_accessed=bytes_accessed, transcendentals=0
        ),
    )


def sheet_substep(water, current_rows, inflow_anode, inflow_cathode):
    diffusivity = base_diffusion + slope_diffusion * water
    face_z = (
        -0.5 * (diffusivity[1:] + diffusivity[:-1]) * (water[1:] - water[:-1])
        + drag_rate * current_rows[None] * water[:-1]
    )
    change = jnp.concatenate([inflow_anode[None], face_z]) - jnp.concatenate(
        [face_z, -inflow_cathode[None]]
    )
    return water + change


def ring(axis, shift):
    count = lax.axis_size(axis)
    return [(i, (i + shift) % count) for i in range(count)]


def on_device(populations, solid_mask, water_sheet, current):
    lattice = populations[0]
    solids = solid_mask[0]
    layers, height, width = lattice.shape[1:]
    groups = lax.axis_size(("side", "gy"))
    gy_count = lax.axis_size("gy")
    sub = width // groups
    f32 = jnp.float32
    mask_values = solids.astype(f32)[None]

    def rows_of(cut):
        return jnp.concatenate([lattice[:, :, cut], mask_values[:, :, cut]])

    low = lax.ppermute(rows_of(slice(height - HALO, height)), "gx", ring("gx", 1))
    high = lax.ppermute(rows_of(slice(0, HALO)), "gx", ring("gx", -1))

    strip = jax.ShapeDtypeStruct((DIRS + 1, height // 2, LANES), f32)
    send_left, send_right = pl.pallas_call(
        strip_kernel, out_shape=(strip, strip),
        in_specs=[VMEM, VMEM], out_specs=(VMEM, VMEM),
    )(lattice, solids)
    left = lax.ppermute(send_right, "gy", ring("gy", 1))
    right = lax.ppermute(send_left, "gy", ring("gy", -1))

    surface = jnp.sum(lattice[:, 0], axis=0)
    ends = jnp.stack([water_sheet[0], water_sheet[-1]])
    own = ends.reshape(2, height, gy_count, sub).transpose(0, 2, 1, 3)
    me = lax.axis_index(("side", "gy"))
    extra = jnp.where(me < groups // 2, jnp.roll(own, -1, axis=1), jnp.roll(own, 1, axis=1))
    to_sheet = surface.reshape(height, groups, sub).transpose(1, 0, 2)
    payload = jnp.stack(
        [own.reshape(groups, height, sub), extra.reshape(groups, height, sub), to_sheet], axis=1
    ).reshape(groups, 3 * height * sub // LANES, LANES)
    got = lax.all_to_all(payload, ("side", "gy"), split_axis=0, concat_axis=0, tiled=True)
    got = got.reshape(groups, 3, height, sub)
    water_here = got[:, :2].transpose(1, 2, 0, 3).reshape(2, height, width)
    halves = got[:, 2].reshape(2, gy_count, height, sub).transpose(0, 2, 1, 3)
    halves = halves.reshape(2, height, gy_count * sub)
    inflow_anode = uptake_rate * (uptake(halves[0]) - water_sheet[0])
    inflow_cathode = uptake_rate * (uptake(halves[1]) - water_sheet[-1])
    water = water_sheet
    for repeat in range(SUBSTEPS):
        water = sheet_substep(water, current, inflow_anode, inflow_cathode)

    corner = jax.ShapeDtypeStruct((DIRS + 3, HALO, LANES), f32)
    send_up, send_down = pl.pallas_call(
        corner_kernel, out_shape=(corner, corner),
        in_specs=[VMEM] * 3, out_specs=(VMEM, VMEM),
    )(left, right, water_here)
    corner_low = lax.ppermute(send_up, "gx", ring("gx", 1))
    corner_high = lax.ppermute(send_down, "gx", ring("gx", -1))

    window = height + 2 * HALO
    result = jax.ShapeDtypeStruct(lattice.shape, f32)
    cost = pl.CostEstimate(flops=200 * 8 * 4 * 52 * 128, bytes_accessed=8 << 20, transcendentals=0)
    middle = pl.pallas_call(
        middle_kernel, out_shape=result, in_specs=[VMEM] * 7, out_specs=VMEM,
        scratch_shapes=window_scratch(layers, window), cost_estimate=cost,
    )(lattice, solids, water_here, low, high, corner_low, corner_high)
    out = pl.pallas_call(
        edge_kernel, out_shape=result, in_specs=[VMEM] * 10, out_specs=VMEM,
        scratch_shapes=window_scratch(layers, window), cost_estimate=cost,
    )(lattice, solids, water_here, low, high, left, right, corner_low, corner_high, middle)
    return (out[None], water)


def solution(mesh):
    in_specs = (
        P("side", None, None, "gx", "gy"),
        P("side", None, "gx", "gy"),
        P(None, "gx", ("side", "gy")),
        P("gx", ("side", "gy")),
    )
    out_specs = (P("side", None, None, "gx", "gy"), P(None, "gx", ("side", "gy")))
    return jax.shard_map(
        on_device, mesh=mesh, in_specs=in_specs, out_specs=out_specs, check_vma=False
    )
```

```python
import functools

import jax
import jax.numpy as jnp
from jax import lax
from jax.experimental import pallas as pl
from jax.experimental.pallas import tpu as pltpu
from jax.sharding import PartitionSpec as P

STEPS = 8
SUBSTEPS = 2
HALO = 2 * STEPS
TILE = 8
LANES = 128

velocity_table = (
    (0, 0, 0),
    (1, 0, 0),
    (-1, 0, 0),
    (0, 1, 0),
    (0, -1, 0),
    (0, 0, 1),
    (0, 0, -1),
    (1, 1, 0),
    (-1, -1, 0),
    (1, -1, 0),
    (-1, 1, 0),
    (1, 0, 1),
    (-1, 0, -1),
    (1, 0, -1),
    (-1, 0, 1),
    (0, 1, 1),
    (0, -1, -1),
    (0, 1, -1),
    (0, -1, 1),
)
DIRS = len(velocity_table)
wall_potential = 0.4
uptake_rate = 0.02
drag_rate = 0.03
base_diffusion = 0.05
slope_diffusion = 0.015
ROOT2 = 2.0**0.5

VMEM = pl.BlockSpec(memory_space=pltpu.VMEM)


def uptake(density_row):
    activity = density_row / (1.0 + density_row)
    return 0.043 + activity * (17.18 + activity * (-39.85 + 36.0 * activity))


def spin(tile, shift):
    shift = shift % LANES
    return tile if shift == 0 else pltpu.roll(tile, shift, 1)


def lane_index():
    return lax.broadcasted_iota(jnp.int32, (TILE, LANES), 1)


def set_pairs(values, row, z, even_ref, odd_ref, rest_ref, density_ref, psi_ref, pore):
    rows = pl.ds(row, TILE)
    if rest_ref is not None:
        rest_ref[z, rows, :] = values[0]
    rho = values[0]
    partial = []
    for k in range(9):
        one, two = values[2 * k + 1], values[2 * k + 2]
        both = one + two
        even_ref[k, z, rows, :] = both
        odd_ref[k, z, rows, :] = one - two
        partial.append(both)
    while len(partial) > 1:
        partial = [a + b for a, b in zip(partial[::2], partial[1::2])] + (
            [partial[-1]] if len(partial) % 2 else []
        )
    rho = rho + partial[0]
    density_ref[z, rows, :] = rho
    psi_ref[z, rows, :] = jnp.where(pore > 0.5, 1.0 - jnp.exp(-rho), wall_potential)
    return rho


def run_steps(refs, layers, window_rows):
    (posts, sets, pull_ref, pore_ref, flux_ref) = refs
    spare = window_rows + 2 * TILE

    def across(values, z, sign):
        above = values[z + 1] if z + 1 < layers else None
        below = values[z - 1] if z > 0 else None
        if above is None and below is None:
            return jnp.zeros((TILE, LANES), jnp.float32)
        if above is None:
            return below if sign > 0 else -below
        if below is None:
            return above
        return above + below if sign > 0 else above - below

    def gather(row, target):
        even_ref, odd_ref, density_ref, psi_ref = target
        rows = pl.ds(row, TILE)
        for z in range(layers):
            values = []
            for i in range(DIRS):
                _, shift_y, shift_z = velocity_table[i]
                reflected = z - shift_z < 0 or z - shift_z >= layers
                values.append(spin(posts[i, z, rows, :], 0 if reflected else shift_y))
            set_pairs(values, row, z, even_ref, odd_ref, None, density_ref, psi_ref, pore_ref[z, rows, :])

    def pull(row, source):
        psi_ref = source[3]
        rows = pl.ds(row, TILE)
        centre = [psi_ref[z, rows, :] for z in range(layers)]
        plus = [psi_ref[z, pl.ds(row + 1, TILE), :] for z in range(layers)]
        minus = [psi_ref[z, pl.ds(row - 1, TILE), :] for z in range(layers)]
        slope = [a - b for a, b in zip(plus, minus)]
        pair = [a + b for a, b in zip(plus, minus)]
        for z in range(layers):
            lift = across(centre, z, -1)
            shell = (centre[z] + centre[z]) + pair[z] + across(centre, z, 1)
            pull_ref[0, z, rows, :] = (
                (slope[z] + slope[z]) + across(slope, z, 1) + (spin(slope[z], 1) + spin(slope[z], -1))
            )
            pull_ref[1, z, rows, :] = spin(shell, -1) - spin(shell, 1)
            pull_ref[2, z, rows, :] = (
                (lift + lift) + across(pair, z, -1) + (spin(lift, 1) + spin(lift, -1))
            )

    def collide(row, source):
        even_ref, odd_ref, density_ref, psi_ref = source
        rows = pl.ds(row, TILE)
        for z in range(layers):
            rho = density_ref[z, rows, :]
            is_pore = pore_ref[z, rows, :] > 0.5
            delta = [None] + [odd_ref[k, z, rows, :] for k in range(9)]
            pulled = psi_ref[z, rows, :] * (1.0 / 15.0)
            scale = jnp.where(is_pore, (3.0 / ROOT2) / rho, 0.0)
            u = []
            for component in range(3):
                value = None
                for k in range(1, 10):
                    factor = velocity_table[2 * k - 1][component]
                    if factor:
                        if value is None:
                            value = delta[k]
                        else:
                            value = value + delta[k] if factor > 0 else value - delta[k]
                u.append((value + pulled * pull_ref[component, z, rows, :]) * scale)
            base = 1.0 - (u[0] * u[0] + u[1] * u[1] + u[2] * u[2]) * (1.0 / 3.0)
            a_diag = jnp.where(is_pore, rho * (1.25 / 36.0), 0.0)
            a_axis = a_diag + a_diag
            o_diag = a_diag * ROOT2
            o_axis = a_axis * ROOT2
            keep_even = jnp.where(is_pore, -0.125, 0.5)
            keep_odd = jnp.where(is_pore, -0.125, -0.5)
            posts[0, z, rows, :] = posts[0, z, rows, :] * (keep_even + keep_even) + base * (a_diag * 12.0)
            for k in range(1, 10):
                i = 2 * k - 1
                e = velocity_table[i]
                along = None
                for component in range(3):
                    if e[component] == 0:
                        continue
                    if along is None:
                        along = u[component]
                    elif e[component] > 0:
                        along = along + u[component]
                    else:
                        along = along - u[component]
                axis = k <= 3
                even = even_ref[k - 1, z, rows, :] * keep_even + (along * along + base) * (
                    a_axis if axis else a_diag
                )
                odd = delta[k] * keep_odd + along * (o_axis if axis else o_diag)
                for j, sign, post in ((i, 1, even + odd), (i + 1, -1, even - odd)):
                    other = i + 1 if j == i else i
                    shift_x, shift_y, shift_z = (sign * v for v in e)
                    if z + shift_z < 0:
                        inflow = flux_ref[rows, :] * (1.0 / 3.0 if axis else 1.0 / 6.0)
                        posts[other, z, rows, :] = post - inflow
                    elif z + shift_z >= layers:
                        posts[other, z, rows, :] = post
                    else:
                        posts[j, z + shift_z, pl.ds(row + shift_x, TILE), :] = post

    def tiles_of(step):
        return (window_rows - 2 - 4 * step + TILE - 1) // TILE

    def two_steps(pair, carry):
        for half in range(2):
            step = 2 * pair + half
            first = 2 * step + 1
            here, there = sets[half], sets[1 - half]
            before = step - 1
            last = jnp.where(step == 0, spare, 2 * before + TILE * (tiles_of(before) - 1))
            gather(last, here)
            pull(first, here)
            pull(first + TILE, here)
            collide(first, here)

            def turn(tile, inner, first=first, here=here, there=there):
                row = first + TILE * tile
                pull(row + TILE, here)
                gather(row - 1 - TILE, there)
                collide(row, here)
                return inner

            lax.fori_loop(1, tiles_of(step), turn, 0)
        return carry

    lax.fori_loop(0, STEPS // 2, two_steps, 0)
    gather(2 * (STEPS - 1) + TILE * (tiles_of(STEPS - 1) - 1), sets[STEPS % 2])


def start_flux(rho, row, flux_ref):
    rows = pl.ds(row, TILE)
    flux_ref[rows, :] = uptake_rate * (uptake(rho) - flux_ref[rows, :])


def begin(read, read_pore, row, layers, refs):
    (posts, sets, pull_ref, pore_ref, flux_ref) = refs
    even_ref, odd_ref, density_ref, psi_ref = sets[0]
    for z in range(layers):
        pore = read_pore(z)
        pore_ref[z, pl.ds(row, TILE), :] = pore
        values = [read(i, z) for i in range(DIRS)]
        rho = set_pairs(values, row, z, even_ref, odd_ref, posts.at[0], density_ref, psi_ref, pore)
        if z == 0:
            start_flux(rho, row, flux_ref)


def finish(write, refs, layers, height):
    (posts, sets, pull_ref, pore_ref, flux_ref) = refs
    even_ref, odd_ref = sets[STEPS % 2][:2]

    def tile_out(t, carry):
        rows = pl.ds(HALO + TILE * t, TILE)
        for z in range(layers):
            write(0, z, t, posts[0, z, rows, :])
            for k in range(9):
                even, odd = even_ref[k, z, rows, :], odd_ref[k, z, rows, :]
                write(2 * k + 1, z, t, (even + odd) * 0.5)
                write(2 * k + 2, z, t, (even - odd) * 0.5)
        return carry

    lax.fori_loop(0, height // TILE, tile_out, 0)


def regroup(scratch):
    posts, e0, o0, d0, p0, e1, o1, d1, p1, pull_ref, pore_ref, flux_ref = scratch
    return posts, ((e0, o0, d0, p0), (e1, o1, d1, p1)), pull_ref, pore_ref, flux_ref


def window_scratch(layers, rows):
    padded = rows + 3 * TILE

    def one(*lead):
        return pltpu.VMEM(lead + (padded, LANES), jnp.float32)

    state = [one(9, layers), one(9, layers), one(layers), one(layers)]
    return [one(DIRS, layers)] + state + state + [one(3, layers), one(layers), one()]


def middle_kernel(f_ref, mask_ref, water_ref, low_ref, high_ref, clow_ref, chigh_ref, out_ref, *scratch):
    refs = regroup(scratch)
    flux_ref = refs[4]
    layers, height = f_ref.shape[1], f_ref.shape[2]
    flux_ref[:HALO, :] = clow_ref[DIRS + 1]
    flux_ref[HALO : HALO + height, :] = water_ref[0]
    flux_ref[HALO + height : 2 * HALO + height, :] = chigh_ref[DIRS + 1]

    def outer(ref, start):
        def tile_in(t, carry):
            rows = pl.ds(pl.multiple_of(TILE * t, TILE), TILE)
            begin(lambda i, z: ref[i, z, rows, :], lambda z: ref[DIRS, z, rows, :], start + TILE * t, layers, refs)
            return carry

        lax.fori_loop(0, HALO // TILE, tile_in, 0)

    outer(low_ref, 0)

    def tile_in(t, carry):
        rows = pl.ds(pl.multiple_of(TILE * t, TILE), TILE)
        begin(lambda i, z: f_ref[i, z, rows, :], lambda z: mask_ref[z, rows, :].astype(jnp.float32),
              HALO + TILE * t, layers, refs)
        return carry

    lax.fori_loop(0, height // TILE, tile_in, 0)
    outer(high_ref, HALO + height)
    run_steps(refs, layers, height + 2 * HALO)

    def write(i, z, t, value):
        out_ref[i, z, pl.ds(pl.multiple_of(TILE * t, TILE), TILE), :] = value

    finish(write, refs, layers, height)


def edge_kernel(f_ref, mask_ref, water_ref, low_ref, high_ref, left_ref, right_ref, clow_ref,
                chigh_ref, middle_ref, out_ref, *scratch):
    refs = regroup(scratch)
    flux_ref = refs[4]
    layers, height = f_ref.shape[1], f_ref.shape[2]
    lane = lane_index()
    move = 3 * HALO
    left_at = 2 * HALO
    low_tiles = HALO // TILE
    mid_tiles = height // TILE
    half_tiles = mid_tiles // 2
    half_lanes = LANES // 2
    at_end = lane >= LANES - 2 * HALO
    at_left = (lane >= left_at) & (lane < left_at + HALO)
    at_right = lane < HALO

    def join(own, left, right):
        return jnp.where(at_end, own, jnp.where(at_right, right, jnp.where(at_left, left, spin(own, move))))

    for tile in range(2 * low_tiles + mid_tiles):
        if low_tiles <= tile < low_tiles + mid_tiles:
            t = tile - low_tiles
            own_rows = slice(TILE * t, TILE * (t + 1))
            rows = slice(TILE * (t % half_tiles), TILE * (t % half_tiles) + TILE)
            first = half_lanes * (t // half_tiles)

            def halo(i, z, rows=rows, first=first):
                at = first + HALO * z
                return spin(left_ref[i, rows, :], left_at - at), spin(right_ref[i, rows, :], -at)

            def read(i, z, own_rows=own_rows, halo=halo):
                return join(f_ref[i, z, own_rows, :], *halo(i, z))

            def read_pore(z, own_rows=own_rows, halo=halo):
                return join(mask_ref[z, own_rows, :].astype(jnp.float32), *halo(DIRS, z))

            own, extra = (water_ref[k, own_rows, :] for k in range(2))
        else:
            t = tile if tile < low_tiles else tile - low_tiles - mid_tiles
            own_ref, corner_ref = (low_ref, clow_ref) if tile < low_tiles else (high_ref, chigh_ref)
            rows = slice(TILE * t, TILE * (t + 1))

            def read(i, z, rows=rows, own_ref=own_ref, corner_ref=corner_ref):
                both = corner_ref[i, rows, :]
                return join(own_ref[i, z, rows, :], spin(both, left_at - HALO * z),
                            spin(both, -half_lanes - HALO * z))

            def read_pore(z, read=read):
                return read(DIRS, z)

            own, extra = (corner_ref[DIRS + 1 + k, rows, :] for k in range(2))
        flux_ref[TILE * tile : TILE * (tile + 1), :] = join(own, spin(extra, move), extra)
        begin(read, read_pore, TILE * tile, layers, refs)
    run_steps(refs, layers, height + 2 * HALO)
    inside = (lane >= HALO) & (lane < LANES - HALO)

    def write(i, z, t, value):
        rows = pl.ds(pl.multiple_of(TILE * t, TILE), TILE)
        edge = jnp.where(lane < half_lanes, spin(value, -move), value)
        out_ref[i, z, rows, :] = jnp.where(inside, middle_ref[i, z, rows, :], edge)

    finish(write, refs, layers, height)


def strip_kernel(f_ref, mask_ref, left_ref, right_ref):
    layers, height = f_ref.shape[1], f_ref.shape[2]
    lane = lane_index()
    half_rows = height // 2
    half_lanes = LANES // 2

    def pack(i, read):
        for t in range(half_rows // TILE):
            rows = slice(TILE * t, TILE * (t + 1))
            first = last = None
            for h in range(2):
                for z in range(layers):
                    tile = read(z, slice(half_rows * h + TILE * t, half_rows * h + TILE * (t + 1)))
                    at = half_lanes * h + HALO * z
                    one = spin(tile, at)
                    two = spin(tile, at + HALO)
                    mine = lane >= at
                    first = one if first is None else jnp.where(mine, one, first)
                    last = two if last is None else jnp.where(mine, two, last)
            left_ref[i, rows, :] = first
            right_ref[i, rows, :] = last

    for i in range(DIRS):
        pack(i, lambda z, rows, i=i: f_ref[i, z, rows, :])
    pack(DIRS, lambda z, rows: mask_ref[z, rows, :].astype(jnp.float32))


def corner_kernel(left_ref, right_ref, water_ref, up_ref, down_ref):
    half_lanes = LANES // 2
    lane = lane_index()
    tiles = left_ref.shape[1] // TILE

    for i in range(DIRS + 1):
        for t in range(tiles):
            rows = slice(TILE * t, TILE * (t + 1))
            left, right = left_ref[i, rows, :], right_ref[i, rows, :]
            up_ref[i, rows, :] = jnp.where(lane < half_lanes, spin(left, half_lanes), right)
            down_ref[i, rows, :] = jnp.where(lane < half_lanes, left, spin(right, half_lanes))
    height = water_ref.shape[1]
    for k in range(2):
        up_ref[DIRS + 1 + k] = water_ref[k, height - HALO :, :]
        down_ref[DIRS + 1 + k] = water_ref[k, :HALO, :]


def sheet_substep(water, current_rows, inflow_anode, inflow_cathode):
    diffusivity = base_diffusion + slope_diffusion * water
    face_z = (
        -0.5 * (diffusivity[1:] + diffusivity[:-1]) * (water[1:] - water[:-1])
        + drag_rate * current_rows[None] * water[:-1]
    )
    change = jnp.concatenate([inflow_anode[None], face_z]) - jnp.concatenate(
        [face_z, -inflow_cathode[None]]
    )
    return water + change


def ring(axis, shift):
    count = lax.axis_size(axis)
    return [(i, (i + shift) % count) for i in range(count)]


def on_device(populations, solid_mask, water_sheet, current):
    lattice = populations[0]
    solids = solid_mask[0]
    layers, height, width = lattice.shape[1:]
    groups = lax.axis_size(("side", "gy"))
    gy_count = lax.axis_size("gy")
    sub = width // groups
    f32 = jnp.float32
    mask_values = solids.astype(f32)[None]

    def rows_of(cut):
        return jnp.concatenate([lattice[:, :, cut], mask_values[:, :, cut]])

    low = lax.ppermute(rows_of(slice(height - HALO, height)), "gx", ring("gx", 1))
    high = lax.ppermute(rows_of(slice(0, HALO)), "gx", ring("gx", -1))

    strip = jax.ShapeDtypeStruct((DIRS + 1, height // 2, LANES), f32)
    send_left, send_right = pl.pallas_call(
        strip_kernel, out_shape=(strip, strip),
        in_specs=[VMEM, VMEM], out_specs=(VMEM, VMEM),
    )(lattice, solids)
    left = lax.ppermute(send_right, "gy", ring("gy", 1))
    right = lax.ppermute(send_left, "gy", ring("gy", -1))

    surface = jnp.sum(lattice[:, 0], axis=0)
    ends = jnp.stack([water_sheet[0], water_sheet[-1]])
    own = ends.reshape(2, height, gy_count, sub).transpose(0, 2, 1, 3)
    me = lax.axis_index(("side", "gy"))
    extra = jnp.where(me < groups // 2, jnp.roll(own, -1, axis=1), jnp.roll(own, 1, axis=1))
    to_sheet = surface.reshape(height, groups, sub).transpose(1, 0, 2)
    payload = jnp.stack(
        [own.reshape(groups, height, sub), extra.reshape(groups, height, sub), to_sheet], axis=1
    ).reshape(groups, 3 * height * sub // LANES, LANES)
    got = lax.all_to_all(payload, ("side", "gy"), split_axis=0, concat_axis=0, tiled=True)
    got = got.reshape(groups, 3, height, sub)
    water_here = got[:, :2].transpose(1, 2, 0, 3).reshape(2, height, width)
    halves = got[:, 2].reshape(2, gy_count, height, sub).transpose(0, 2, 1, 3)
    halves = halves.reshape(2, height, gy_count * sub)
    inflow_anode = uptake_rate * (uptake(halves[0]) - water_sheet[0])
    inflow_cathode = uptake_rate * (uptake(halves[1]) - water_sheet[-1])
    water = water_sheet
    for repeat in range(SUBSTEPS):
        water = sheet_substep(water, current, inflow_anode, inflow_cathode)

    corner = jax.ShapeDtypeStruct((DIRS + 3, HALO, LANES), f32)
    send_up, send_down = pl.pallas_call(
        corner_kernel, out_shape=(corner, corner),
        in_specs=[VMEM] * 3, out_specs=(VMEM, VMEM),
    )(left, right, water_here)
    corner_low = lax.ppermute(send_up, "gx", ring("gx", 1))
    corner_high = lax.ppermute(send_down, "gx", ring("gx", -1))

    window = height + 2 * HALO
    result = jax.ShapeDtypeStruct(lattice.shape, f32)
    cost = pl.CostEstimate(flops=200 * 8 * 4 * 52 * 128, bytes_accessed=8 << 20, transcendentals=0)
    middle = pl.pallas_call(
        middle_kernel, out_shape=result, in_specs=[VMEM] * 7, out_specs=VMEM,
        scratch_shapes=window_scratch(layers, window), cost_estimate=cost,
    )(lattice, solids, water_here, low, high, corner_low, corner_high)
    out = pl.pallas_call(
        edge_kernel, out_shape=result, in_specs=[VMEM] * 10, out_specs=VMEM,
        scratch_shapes=window_scratch(layers, window), cost_estimate=cost,
    )(lattice, solids, water_here, low, high, left, right, corner_low, corner_high, middle)
    return (out[None], water)


def solution(mesh):
    in_specs = (
        P("side", None, None, "gx", "gy"),
        P("side", None, "gx", "gy"),
        P(None, "gx", ("side", "gy")),
        P("gx", ("side", "gy")),
    )
    out_specs = (P("side", None, None, "gx", "gy"), P(None, "gx", ("side", "gy")))
    return jax.shard_map(
        on_device, mesh=mesh, in_specs=in_specs, out_specs=out_specs, check_vma=False
    )
```

```python
import jax
import jax.numpy as jnp
from jax import lax
from jax.experimental import pallas as pl
from jax.experimental.pallas import tpu as pltpu
from jax.sharding import PartitionSpec as P


STEPS = 8
SUBSTEPS = 2
HALO = 2 * STEPS
TILE = 8
LANES = 128
WINDOWS = 2

velocity_table = (
    (0, 0, 0),
    (1, 0, 0),
    (-1, 0, 0),
    (0, 1, 0),
    (0, -1, 0),
    (0, 0, 1),
    (0, 0, -1),
    (1, 1, 0),
    (-1, -1, 0),
    (1, -1, 0),
    (-1, 1, 0),
    (1, 0, 1),
    (-1, 0, -1),
    (1, 0, -1),
    (-1, 0, 1),
    (0, 1, 1),
    (0, -1, -1),
    (0, 1, -1),
    (0, -1, 1),
)
DIRS = len(velocity_table)
wall_potential = 0.4
uptake_rate = 0.02
drag_rate = 0.03
base_diffusion = 0.05
slope_diffusion = 0.015
ROOT2 = 2.0**0.5

VMEM = pl.BlockSpec(memory_space=pltpu.VMEM)


def uptake(density_row):
    activity = density_row / (1.0 + density_row)
    return 0.043 + activity * (17.18 + activity * (-39.85 + 36.0 * activity))


def spin(tile, shift):
    shift = shift % LANES
    return tile if shift == 0 else pltpu.roll(tile, shift, 1)


def lane_index():
    return lax.broadcasted_iota(jnp.int32, (TILE, LANES), 1)


def set_pairs(values, row, z, even_ref, odd_ref, rest_ref, density_ref, psi_ref, pore):
    rows = pl.ds(row, TILE)
    if rest_ref is not None:
        rest_ref[z, rows, :] = values[0]
    rho = values[0]
    partial = []
    for k in range(9):
        one, two = values[2 * k + 1], values[2 * k + 2]
        both = one + two
        even_ref[k, z, rows, :] = both
        odd_ref[k, z, rows, :] = one - two
        partial.append(both)
    while len(partial) > 1:
        partial = [a + b for a, b in zip(partial[::2], partial[1::2])] + (
            [partial[-1]] if len(partial) % 2 else []
        )
    rho = rho + partial[0]
    density_ref[z, rows, :] = rho
    psi_ref[z, rows, :] = jnp.where(pore > 0.5, 1.0 - jnp.exp(-rho), wall_potential)
    return rho


def run_steps(refs, layers, window_rows):
    (posts, sets, pull_ref, pore_ref, flux_ref) = refs
    spare = window_rows + 2 * TILE
    planes = [(w * layers, w * layers + z, z) for w in range(WINDOWS) for z in range(layers)]

    def across(values, base, z, sign):
        above = values[base + z + 1] if z + 1 < layers else None
        below = values[base + z - 1] if z > 0 else None
        if above is None and below is None:
            return jnp.zeros((TILE, LANES), jnp.float32)
        if above is None:
            return below if sign > 0 else -below
        if below is None:
            return above
        return above + below if sign > 0 else above - below

    def gather(row, target):
        even_ref, odd_ref, density_ref, psi_ref = target
        rows = pl.ds(row, TILE)
        for base, p, z in planes:
            values = []
            for i in range(DIRS):
                _, shift_y, shift_z = velocity_table[i]
                reflected = z - shift_z < 0 or z - shift_z >= layers
                values.append(spin(posts[i, p, rows, :], 0 if reflected else shift_y))
            set_pairs(values, row, p, even_ref, odd_ref, None, density_ref, psi_ref, pore_ref[p, rows, :])

    def pull(row, source):
        psi_ref = source[3]
        rows = pl.ds(row, TILE)
        centre = [psi_ref[p, rows, :] for _, p, _ in planes]
        plus = [psi_ref[p, pl.ds(row + 1, TILE), :] for _, p, _ in planes]
        minus = [psi_ref[p, pl.ds(row - 1, TILE), :] for _, p, _ in planes]
        slope = [a - b for a, b in zip(plus, minus)]
        pair = [a + b for a, b in zip(plus, minus)]
        for base, p, z in planes:
            lift = across(centre, base, z, -1)
            shell = (centre[p] + centre[p]) + pair[p] + across(centre, base, z, 1)
            pull_ref[0, p, rows, :] = (
                (slope[p] + slope[p]) + across(slope, base, z, 1) + (spin(slope[p], 1) + spin(slope[p], -1))
            )
            pull_ref[1, p, rows, :] = spin(shell, -1) - spin(shell, 1)
            pull_ref[2, p, rows, :] = (
                (lift + lift) + across(pair, base, z, -1) + (spin(lift, 1) + spin(lift, -1))
            )

    def collide(row, source):
        even_ref, odd_ref, density_ref, psi_ref = source
        rows = pl.ds(row, TILE)
        for base, p, z in planes:
            rho = density_ref[p, rows, :]
            is_pore = pore_ref[p, rows, :] > 0.5
            delta = [None] + [odd_ref[k, p, rows, :] for k in range(9)]
            pulled = psi_ref[p, rows, :] * (1.0 / 15.0)
            scale = jnp.where(is_pore, (3.0 / ROOT2) / rho, 0.0)
            u = []
            for component in range(3):
                value = None
                for k in range(1, 10):
                    factor = velocity_table[2 * k - 1][component]
                    if factor:
                        if value is None:
                            value = delta[k]
                        else:
                            value = value + delta[k] if factor > 0 else value - delta[k]
                u.append((value + pulled * pull_ref[component, p, rows, :]) * scale)
            base = 1.0 - (u[0] * u[0] + u[1] * u[1] + u[2] * u[2]) * (1.0 / 3.0)
            a_diag = jnp.where(is_pore, rho * (1.25 / 36.0), 0.0)
            a_axis = a_diag + a_diag
            o_diag = a_diag * ROOT2
            o_axis = a_axis * ROOT2
            keep_even = jnp.where(is_pore, -0.125, 0.5)
            keep_odd = jnp.where(is_pore, -0.125, -0.5)
            posts[0, p, rows, :] = posts[0, p, rows, :] * (keep_even + keep_even) + base * (a_diag * 12.0)
            for k in range(1, 10):
                i = 2 * k - 1
                e = velocity_table[i]
                along = None
                for component in range(3):
                    if e[component] == 0:
                        continue
                    if along is None:
                        along = u[component]
                    elif e[component] > 0:
                        along = along + u[component]
                    else:
                        along = along - u[component]
                axis = k <= 3
                even = even_ref[k - 1, p, rows, :] * keep_even + (along * along + base) * (
                    a_axis if axis else a_diag
                )
                odd = delta[k] * keep_odd + along * (o_axis if axis else o_diag)
                for j, sign, post in ((i, 1, even + odd), (i + 1, -1, even - odd)):
                    other = i + 1 if j == i else i
                    shift_x, _, shift_z = (sign * v for v in e)
                    if z + shift_z < 0:
                        inflow = flux_ref[p // layers, rows, :] * (1.0 / 3.0 if axis else 1.0 / 6.0)
                        posts[other, p, rows, :] = post - inflow
                    elif z + shift_z >= layers:
                        posts[other, p, rows, :] = post
                    else:
                        posts[j, p + shift_z, pl.ds(row + shift_x, TILE), :] = post

    def tiles_of(step):
        return (window_rows - 2 - 4 * step + TILE - 1) // TILE

    def two_steps(pair, carry):
        for half in range(2):
            step = 2 * pair + half
            first = 2 * step + 1
            here, there = sets[half], sets[1 - half]
            before = step - 1
            last = jnp.where(step == 0, spare, 2 * before + TILE * (tiles_of(before) - 1))
            gather(last, here)
            pull(first, here)
            pull(first + TILE, here)
            collide(first, here)

            def turn(tile, inner, first=first, here=here, there=there):
                row = first + TILE * tile
                pull(row + TILE, here)
                gather(row - 1 - TILE, there)
                collide(row, here)
                return inner

            lax.fori_loop(1, tiles_of(step), turn, 0)
        return carry

    lax.fori_loop(0, STEPS // 2, two_steps, 0)
    gather(2 * (STEPS - 1) + TILE * (tiles_of(STEPS - 1) - 1), sets[STEPS % 2])


def begin(read, read_pore, row, window, layers, refs):
    (posts, sets, _, pore_ref, flux_ref) = refs
    even_ref, odd_ref, density_ref, psi_ref = sets[0]
    rows = pl.ds(row, TILE)
    for z in range(layers):
        p = window * layers + z
        pore = read_pore(z)
        pore_ref[p, rows, :] = pore
        values = [read(i, z) for i in range(DIRS)]
        rho = set_pairs(values, row, p, even_ref, odd_ref, posts.at[0], density_ref, psi_ref, pore)
        if z == 0:
            flux_ref[window, rows, :] = uptake_rate * (uptake(rho) - flux_ref[window, rows, :])


def finish(out_ref, refs, layers, height):
    (posts, sets, _, _, _) = refs
    even_ref, odd_ref = sets[STEPS % 2][:2]
    lane = lane_index()
    inside = (lane >= HALO) & (lane < LANES - HALO)
    move = 3 * HALO

    def tile_out(t, carry):
        rows = pl.ds(HALO + TILE * t, TILE)
        to = pl.ds(pl.multiple_of(TILE * t, TILE), TILE)

        def join(read):
            middle, edge = read(0), read(1)
            edge = jnp.where(lane < LANES // 2, spin(edge, -move), edge)
            return jnp.where(inside, middle, edge)

        for z in range(layers):
            out_ref[0, z, to, :] = join(lambda w: posts[0, w * layers + z, rows, :])
            for k in range(9):
                even = join(lambda w: even_ref[k, w * layers + z, rows, :]) * 0.5
                odd = join(lambda w: odd_ref[k, w * layers + z, rows, :]) * 0.5
                out_ref[2 * k + 1, z, to, :] = even + odd
                out_ref[2 * k + 2, z, to, :] = even - odd
        return carry

    lax.fori_loop(0, height // TILE, tile_out, 0)


def window_scratch(layers, rows):
    padded = rows + 3 * TILE
    planes = WINDOWS * layers

    def one(*lead):
        return pltpu.VMEM(lead + (padded, LANES), jnp.float32)

    state = [one(9, planes), one(9, planes), one(planes), one(planes)]
    return [one(DIRS, planes)] + state + state + [one(3, planes), one(planes), one(WINDOWS)]


def lattice_kernel(f_ref, mask_ref, water_ref, low_ref, high_ref, left_ref, right_ref, clow_ref,
                   chigh_ref, out_ref, *scratch):
    posts, e0, o0, d0, p0, e1, o1, d1, p1, pull_ref, pore_ref, flux_ref = scratch
    refs = posts, ((e0, o0, d0, p0), (e1, o1, d1, p1)), pull_ref, pore_ref, flux_ref
    layers, height = f_ref.shape[1], f_ref.shape[2]
    lane = lane_index()
    move = 3 * HALO
    left_at = 2 * HALO
    low_tiles = HALO // TILE
    mid_tiles = height // TILE
    half_tiles = mid_tiles // 2
    half_lanes = LANES // 2
    at_end = lane >= LANES - 2 * HALO
    at_left = (lane >= left_at) & (lane < left_at + HALO)
    at_right = lane < HALO

    def join(own, left, right):
        return jnp.where(at_end, own, jnp.where(at_right, right, jnp.where(at_left, left, spin(own, move))))

    for tile in range(2 * low_tiles + mid_tiles):
        if low_tiles <= tile < low_tiles + mid_tiles:
            t = tile - low_tiles
            own_rows = slice(TILE * t, TILE * (t + 1))
            rows = slice(TILE * (t % half_tiles), TILE * (t % half_tiles) + TILE)
            first = half_lanes * (t // half_tiles)

            def own_of(i, z, own_rows=own_rows):
                return f_ref[i, z, own_rows, :] if i < DIRS else mask_ref[z, own_rows, :].astype(jnp.float32)

            def halo(i, z, rows=rows, first=first):
                at = first + HALO * z
                return spin(left_ref[i, rows, :], left_at - at), spin(right_ref[i, rows, :], -at)

            own, extra = (water_ref[k, own_rows, :] for k in range(2))
        else:
            t = tile if tile < low_tiles else tile - low_tiles - mid_tiles
            own_ref, corner_ref = (low_ref, clow_ref) if tile < low_tiles else (high_ref, chigh_ref)
            rows = slice(TILE * t, TILE * (t + 1))

            def own_of(i, z, rows=rows, own_ref=own_ref):
                return own_ref[i, z, rows, :]

            def halo(i, z, rows=rows, corner_ref=corner_ref):
                both = corner_ref[i, rows, :]
                return spin(both, left_at - HALO * z), spin(both, -half_lanes - HALO * z)

            own, extra = (corner_ref[DIRS + 1 + k, rows, :] for k in range(2))

        def edge_of(i, z, own_of=own_of, halo=halo):
            return join(own_of(i, z), *halo(i, z))

        flux_ref[0, TILE * tile : TILE * (tile + 1), :] = own
        flux_ref[1, TILE * tile : TILE * (tile + 1), :] = join(own, spin(extra, move), extra)
        begin(own_of, lambda z, f=own_of: f(DIRS, z), TILE * tile, 0, layers, refs)
        begin(edge_of, lambda z, f=edge_of: f(DIRS, z), TILE * tile, 1, layers, refs)
    run_steps(refs, layers, height + 2 * HALO)
    finish(out_ref, refs, layers, height)


def strip_kernel(me_ref, f_ref, mask_ref, ends_ref, left_ref, right_ref, payload_ref):
    layers, height = f_ref.shape[1], f_ref.shape[2]
    lane = lane_index()
    half_rows = height // 2
    half_lanes = LANES // 2

    def pack(i, read):
        for t in range(half_rows // TILE):
            rows = slice(TILE * t, TILE * (t + 1))
            first = last = None
            for h in range(2):
                for z in range(layers):
                    tile = read(z, slice(half_rows * h + TILE * t, half_rows * h + TILE * (t + 1)))
                    at = half_lanes * h + HALO * z
                    one = spin(tile, at)
                    two = spin(tile, at + HALO)
                    mine = lane >= at
                    first = one if first is None else jnp.where(mine, one, first)
                    last = two if last is None else jnp.where(mine, two, last)
            left_ref[i, rows, :] = first
            right_ref[i, rows, :] = last

    for i in range(DIRS):
        pack(i, lambda z, rows, i=i: f_ref[i, z, rows, :])
    pack(DIRS, lambda z, rows: mask_ref[z, rows, :].astype(jnp.float32))

    groups = payload_ref.shape[0]
    peers = groups // 2
    sub = LANES // groups
    tiles = height // TILE
    early = me_ref[0] < peers
    surface = []
    for t in range(tiles):
        rho = f_ref[0, 0, TILE * t : TILE * (t + 1), :]
        for i in range(1, DIRS):
            rho = rho + f_ref[i, 0, TILE * t : TILE * (t + 1), :]
        surface.append(rho)
    for which in range(2):
        ends = [ends_ref[which, TILE * t : TILE * (t + 1), :] for t in range(tiles)]
        for g in range(peers):
            e = which * peers + g
            after, before = (g + 1) % peers, (g + peers - 1) % peers
            water = density = None
            for kind in range(2):
                for t in range(tiles):
                    at = (kind * tiles + t) * sub
                    if kind == 0:
                        piece = spin(ends[t], at - g * sub)
                    else:
                        piece = jnp.where(early, spin(ends[t], at - after * sub), spin(ends[t], at - before * sub))
                    water = piece if water is None else jnp.where(lane >= at, piece, water)
            for t in range(tiles):
                piece = spin(surface[t], (t - e) * sub)
                density = piece if density is None else jnp.where(lane >= t * sub, piece, density)
            payload_ref[e, :TILE, :] = water
            payload_ref[e, TILE:, :] = density


def corner_kernel(got_ref, left_ref, right_ref, up_ref, down_ref, water_ref):
    half_lanes = LANES // 2
    lane = lane_index()
    groups = got_ref.shape[0]
    sub = LANES // groups
    height = water_ref.shape[1]
    tiles = height // TILE
    for kind in range(2):
        for t in range(tiles):
            rows = slice(TILE * t, TILE * (t + 1))
            value = None
            for c in range(groups):
                piece = spin(got_ref[c, :TILE, :], (c - kind * tiles - t) * sub)
                value = piece if value is None else jnp.where(lane >= c * sub, piece, value)
            water_ref[kind, rows, :] = value
            if TILE * t >= height - HALO:
                up_ref[DIRS + 1 + kind, TILE * t - height + HALO : TILE * (t + 1) - height + HALO, :] = value
            if TILE * t < HALO:
                down_ref[DIRS + 1 + kind, rows, :] = value
    for i in range(DIRS + 1):
        for t in range(HALO // TILE):
            rows = slice(TILE * t, TILE * (t + 1))
            left, right = left_ref[i, rows, :], right_ref[i, rows, :]
            up_ref[i, rows, :] = jnp.where(lane < half_lanes, spin(left, half_lanes), right)
            down_ref[i, rows, :] = jnp.where(lane < half_lanes, left, spin(right, half_lanes))


def sheet_kernel(got_ref, sheet_ref, current_ref, out_ref):
    groups = got_ref.shape[0]
    peers = groups // 2
    sub = LANES // groups
    cells, height, columns = sheet_ref.shape
    lane = lane_index()
    for t in range(height // TILE):
        rows = slice(TILE * t, TILE * (t + 1))
        inflow = []
        for which in range(2):
            rho = None
            for g in range(peers):
                piece = spin(got_ref[which * peers + g, TILE:, :], (g - t) * sub)
                rho = piece if rho is None else jnp.where(lane >= g * sub, piece, rho)
            end = sheet_ref[0 if which == 0 else cells - 1, rows, :]
            inflow.append(uptake_rate * (uptake(rho[:, :columns]) - end))
        drag = drag_rate * current_ref[rows, :]
        source = sheet_ref
        for _ in range(SUBSTEPS):
            below = source[0, rows, :]
            spread_below = base_diffusion + slope_diffusion * below
            entering = inflow[0]
            for k in range(cells):
                if k + 1 < cells:
                    above = source[k + 1, rows, :]
                    spread = base_diffusion + slope_diffusion * above
                    leaving = -0.5 * (spread + spread_below) * (above - below) + drag * below
                else:
                    above = spread = None
                    leaving = -inflow[1]
                out_ref[k, rows, :] = below + (entering - leaving)
                below, spread_below, entering = above, spread, leaving
            source = out_ref


def ring(axis, shift):
    count = lax.axis_size(axis)
    return [(i, (i + shift) % count) for i in range(count)]


def on_device(populations, solid_mask, water_sheet, current):
    lattice = populations[0]
    solids = solid_mask[0]
    layers, height, width = lattice.shape[1:]
    groups = lax.axis_size(("side", "gy"))
    f32 = jnp.float32
    mask_values = solids.astype(f32)[None]

    def shape(*dims):
        return jax.ShapeDtypeStruct(dims, f32)

    def rows_of(cut):
        return jnp.concatenate([lattice[:, :, cut], mask_values[:, :, cut]])

    low = lax.ppermute(rows_of(slice(height - HALO, height)), "gx", ring("gx", 1))
    high = lax.ppermute(rows_of(slice(0, HALO)), "gx", ring("gx", -1))

    ends = jnp.stack([water_sheet[0], water_sheet[-1]])
    ends = jnp.pad(ends, ((0, 0), (0, 0), (0, LANES - ends.shape[2])))
    me = lax.axis_index(("side", "gy")).reshape(1)
    strip = shape(DIRS + 1, height // 2, LANES)
    send_left, send_right, payload = pl.pallas_call(
        strip_kernel, out_shape=(strip, strip, shape(groups, 2 * TILE, LANES)),
        in_specs=[pl.BlockSpec(memory_space=pltpu.SMEM), VMEM, VMEM, VMEM], out_specs=(VMEM,) * 3,
        compiler_params=pltpu.CompilerParams(vmem_limit_bytes=8 << 20),
    )(me, lattice, solids, ends)
    left = lax.ppermute(send_right, "gy", ring("gy", 1))
    right = lax.ppermute(send_left, "gy", ring("gy", -1))
    got = lax.all_to_all(payload, ("side", "gy"), split_axis=0, concat_axis=0, tiled=True)

    corner = shape(DIRS + 3, HALO, LANES)
    send_up, send_down, water_here = pl.pallas_call(
        corner_kernel, out_shape=(corner, corner, shape(2, height, width)),
        in_specs=[VMEM] * 3, out_specs=(VMEM,) * 3,
        compiler_params=pltpu.CompilerParams(vmem_limit_bytes=8 << 20),
    )(got, left, right)
    corner_low = lax.ppermute(send_up, "gx", ring("gx", 1))
    corner_high = lax.ppermute(send_down, "gx", ring("gx", -1))
    water = pl.pallas_call(
        sheet_kernel, out_shape=shape(*water_sheet.shape),
        in_specs=[VMEM] * 3, out_specs=VMEM,
        compiler_params=pltpu.CompilerParams(vmem_limit_bytes=8 << 20),
    )(got, water_sheet, current)
    out = pl.pallas_call(
        lattice_kernel, out_shape=shape(*lattice.shape),
        in_specs=[VMEM] * 9, out_specs=VMEM,
        compiler_params=pltpu.CompilerParams(vmem_limit_bytes=36 << 20),
        scratch_shapes=window_scratch(layers, height + 2 * HALO),
        cost_estimate=pl.CostEstimate(flops=1 << 28, bytes_accessed=8 << 20, transcendentals=0),
    )(lattice, solids, water_here, low, high, left, right, corner_low, corner_high)
    return (out[None], water)


def solution(mesh):
    in_specs = (
        P("side", None, None, "gx", "gy"),
        P("side", None, "gx", "gy"),
        P(None, "gx", ("side", "gy")),
        P("gx", ("side", "gy")),
    )
    out_specs = (P("side", None, None, "gx", "gy"), P(None, "gx", ("side", "gy")))
    return jax.shard_map(
        on_device, mesh=mesh, in_specs=in_specs, out_specs=out_specs, check_vma=False
    )
```

```python
import jax
import jax.numpy as jnp
from jax import lax
from jax.experimental import pallas as pl
from jax.experimental.pallas import tpu as pltpu
from jax.sharding import PartitionSpec as P


STEPS = 8
SUBSTEPS = 2
HALO = 2 * STEPS
TILE = 8
FRONT = TILE
LANES = 128
WINDOWS = 2

velocity_table = (
    (0, 0, 0),
    (1, 0, 0),
    (-1, 0, 0),
    (0, 1, 0),
    (0, -1, 0),
    (0, 0, 1),
    (0, 0, -1),
    (1, 1, 0),
    (-1, -1, 0),
    (1, -1, 0),
    (-1, 1, 0),
    (1, 0, 1),
    (-1, 0, -1),
    (1, 0, -1),
    (-1, 0, 1),
    (0, 1, 1),
    (0, -1, -1),
    (0, 1, -1),
    (0, -1, 1),
)
DIRS = len(velocity_table)
wall_potential = 0.4
uptake_rate = 0.02
drag_rate = 0.03
base_diffusion = 0.05
slope_diffusion = 0.015

VMEM = pl.BlockSpec(memory_space=pltpu.VMEM)


def uptake(density_row):
    activity = density_row / (1.0 + density_row)
    return 0.043 + activity * (17.18 + activity * (-39.85 + 36.0 * activity))


def spin(tile, shift):
    shift = shift % LANES
    return tile if shift == 0 else pltpu.roll(tile, shift, 1)


def lane_index():
    return lax.broadcasted_iota(jnp.int32, (TILE, LANES), 1)


def set_pairs(values, row, z, even_ref, odd_ref, rest_ref, density_ref, psi_ref, pore):
    rows = pl.ds(row, TILE)
    if rest_ref is not None:
        rest_ref[z, rows, :] = values[0]
    rho = values[0]
    partial = []
    for k in range(9):
        one, two = values[2 * k + 1], values[2 * k + 2]
        both = one + two
        even_ref[k, z, rows, :] = both
        odd_ref[k, z, rows, :] = one - two
        partial.append(both)
    while len(partial) > 1:
        partial = [a + b for a, b in zip(partial[::2], partial[1::2])] + (
            [partial[-1]] if len(partial) % 2 else []
        )
    rho = rho + partial[0]
    density_ref[z, rows, :] = rho
    psi_ref[z, rows, :] = jnp.where(pore > 0.0, 1.0 - jnp.exp(-rho), wall_potential)
    return rho


def run_steps(refs, layers, window_rows):
    planes = [(0, z, z) for z in range(layers)]

    def across(values, base, z, sign):
        above = values[base + z + 1] if z + 1 < layers else None
        below = values[base + z - 1] if z > 0 else None
        if above is None and below is None:
            return jnp.zeros((TILE, LANES), jnp.float32)
        if above is None:
            return below if sign > 0 else -below
        if below is None:
            return above
        return above + below if sign > 0 else above - below

    def gather(row, window, parity):
        row = row + FRONT
        posts, sets, share_ref = refs[window][:3]
        target = sets[parity]
        even_ref, odd_ref, density_ref, psi_ref = target[:4]
        rows = pl.ds(row, TILE)
        for base, p, z in planes:
            values = []
            for i in range(DIRS):
                _, shift_y, shift_z = velocity_table[i]
                reflected = z - shift_z < 0 or z - shift_z >= layers
                values.append(spin(posts[i, p, rows, :], 0 if reflected else shift_y))
            set_pairs(values, row, p, even_ref, odd_ref, None, density_ref, psi_ref, share_ref[p, rows, :])

    def fold(row, window, parity):
        row = row + FRONT
        _, _, _, psi_ref, around_ref, tilt_ref = refs[window][1][parity]
        rows = pl.ds(row, TILE)
        for base, p, z in planes:
            centre = psi_ref[p, rows, :]
            left, right = spin(centre, 1), spin(centre, -1)
            around_ref[p, rows, :] = (centre + centre) + (left + right)
            tilt_ref[p, rows, :] = right - left

    def collide(row, window, parity):
        row = row + FRONT
        posts, sets, share_ref, even_keep_ref, odd_keep_ref, flux_ref = refs[window]
        even_ref, odd_ref, density_ref, psi_ref, around_ref, tilt_ref = sets[parity]
        rows, up, down = (pl.ds(row + shift, TILE) for shift in (0, 1, -1))
        slope, column, tilt = {}, {}, {}
        for base, p, z in planes:
            for q in range(max(base, p - 1), min(base + layers, p + 2)):
                if q not in slope:
                    plus, minus = psi_ref[q, up, :], psi_ref[q, down, :]
                    slope[q] = plus - minus
                    column[q] = (plus + minus) + around_ref[q, rows, :]
                    tilt[q] = tilt_ref[q, rows, :]
            pulls = (
                (around_ref[p, up, :] - around_ref[p, down, :]) + across(slope, base, z, 1),
                ((tilt[p] + tilt[p]) + (tilt_ref[p, up, :] + tilt_ref[p, down, :]))
                + across(tilt, base, z, 1),
                across(column, base, z, -1),
            )
            rho = density_ref[p, rows, :]
            delta = [None] + [odd_ref[k, p, rows, :] for k in range(9)]
            pulled = psi_ref[p, rows, :] * (1.0 / 15.0)
            a_diag = rho * share_ref[p, rows, :]
            scale = jnp.where(share_ref[p, rows, :] > 0.0, 1.5 / rho, 0.0)
            u = []
            for component in range(3):
                value = None
                for k in range(1, 10):
                    factor = velocity_table[2 * k - 1][component]
                    if factor:
                        if value is None:
                            value = delta[k]
                        else:
                            value = value + delta[k] if factor > 0 else value - delta[k]
                u.append((value + pulled * pulls[component]) * scale)
            b_diag = a_diag - a_diag * ((u[0] * u[0] + u[1] * u[1] + u[2] * u[2]) * (2.0 / 3.0))
            b_axis = b_diag + b_diag
            o_diag = a_diag + a_diag
            o_axis = o_diag + o_diag
            keep_even = even_keep_ref[p, rows, :]
            keep_odd = odd_keep_ref[p, rows, :]
            posts[0, p, rows, :] = posts[0, p, rows, :] * (keep_even + keep_even) + b_diag * 12.0
            for k in range(1, 10):
                i = 2 * k - 1
                e = velocity_table[i]
                along = None
                for component in range(3):
                    if e[component] == 0:
                        continue
                    if along is None:
                        along = u[component]
                    elif e[component] > 0:
                        along = along + u[component]
                    else:
                        along = along - u[component]
                axis = k <= 3
                drift = along * (o_axis if axis else o_diag)
                even = (even_ref[k - 1, p, rows, :] * keep_even + (b_axis if axis else b_diag)) + drift * along
                odd = delta[k] * keep_odd + drift
                for j, sign, post in ((i, 1, even + odd), (i + 1, -1, even - odd)):
                    other = i + 1 if j == i else i
                    shift_x, _, shift_z = (sign * v for v in e)
                    if z + shift_z < 0:
                        inflow = flux_ref[rows, :] * (1.0 / 3.0 if axis else 1.0 / 6.0)
                        posts[other, p, rows, :] = post - inflow
                    elif z + shift_z >= layers:
                        posts[other, p, rows, :] = post
                    else:
                        posts[j, p + shift_z, pl.ds(row + shift_x, TILE), :] = post

    def tiles_of(step):
        return (window_rows - 2 - 4 * step + TILE - 1) // TILE

    for step in range(STEPS):
        half = step % 2
        first = 2 * step + 1
        if step:
            last = 2 * (step - 1) + TILE * (tiles_of(step - 1) - 1)
            for window in range(WINDOWS):
                collide(first, window, half)
            for window in range(WINDOWS):
                fold(last - TILE, window, half)
                gather(last, window, half)
                fold(last, window, half)
        else:
            for window in range(WINDOWS):
                collide(first, window, half)

        def turn(tile, carry, first=first, half=half):
            row = TILE * tile + first
            gather(row - 1 - TILE, 0, 1 - half)
            gather(row - 1 - TILE, 1, 1 - half)
            collide(row, 0, half)
            collide(row, 1, half)
            fold(row - 1 - 2 * TILE, 0, 1 - half)
            fold(row - 1 - 2 * TILE, 1, 1 - half)
            return carry

        lax.fori_loop(1, tiles_of(step), turn, 0)
    for window in range(WINDOWS):
        gather(2 * (STEPS - 1) + TILE * (tiles_of(STEPS - 1) - 1), window, STEPS % 2)


def first_folds(refs, layers, window_rows):
    for tile in range(window_rows // TILE):
        rows = slice(FRONT + TILE * tile, FRONT + TILE * (tile + 1))
        for window in range(WINDOWS):
            psi_ref, around_ref, tilt_ref = refs[window][1][0][3:6]
            for z in range(layers):
                centre = psi_ref[z, rows, :]
                left, right = spin(centre, 1), spin(centre, -1)
                around_ref[z, rows, :] = (centre + centre) + (left + right)
                tilt_ref[z, rows, :] = right - left


def begin(read, read_pore, row, window, layers, refs):
    posts, sets, share_ref, even_keep_ref, odd_keep_ref, flux_ref = refs[window]
    even_ref, odd_ref, density_ref, psi_ref = sets[0][:4]
    row = row + FRONT
    rows = pl.ds(row, TILE)
    for z in range(layers):
        p = z
        pore = read_pore(z)
        is_pore = pore > 0.5
        share_ref[p, rows, :] = jnp.where(is_pore, 1.25 / 36.0, 0.0)
        even_keep_ref[p, rows, :] = jnp.where(is_pore, -0.125, 0.5)
        odd_keep_ref[p, rows, :] = jnp.where(is_pore, -0.125, -0.5)
        values = [read(i, z) for i in range(DIRS)]
        rho = set_pairs(values, row, p, even_ref, odd_ref, posts.at[0], density_ref, psi_ref, pore)
        if z == 0:
            flux_ref[rows, :] = uptake_rate * (uptake(rho) - flux_ref[rows, :])


def finish(out_ref, refs, layers, height):
    lane = lane_index()
    inside = (lane >= HALO) & (lane < LANES - HALO)
    move = 3 * HALO

    def tile_out(t, carry):
        rows = pl.ds(FRONT + HALO + TILE * t, TILE)
        to = pl.ds(pl.multiple_of(TILE * t, TILE), TILE)

        def join(read):
            middle, edge = read(0), read(1)
            edge = jnp.where(lane < LANES // 2, spin(edge, -move), edge)
            return jnp.where(inside, middle, edge)

        for z in range(layers):
            out_ref[0, z, to, :] = join(lambda w: refs[w][0][0, z, rows, :])
            for k in range(9):
                even = join(lambda w: refs[w][1][STEPS % 2][0][k, z, rows, :]) * 0.5
                odd = join(lambda w: refs[w][1][STEPS % 2][1][k, z, rows, :]) * 0.5
                out_ref[2 * k + 1, z, to, :] = even + odd
                out_ref[2 * k + 2, z, to, :] = even - odd
        return carry

    lax.fori_loop(0, height // TILE, tile_out, 0)


def window_scratch(layers, rows):
    padded = FRONT + rows + 2 * TILE

    def one(*lead):
        return pltpu.VMEM(lead + (padded, LANES), jnp.float32)

    state = [one(9, layers), one(9, layers)] + [one(layers)] * 4
    return ([one(DIRS, layers)] + state + state + [one(layers)] * 3 + [one()]) * WINDOWS


def window_refs(scratch):
    count = len(scratch) // WINDOWS
    parts = [scratch[count * w : count * (w + 1)] for w in range(WINDOWS)]
    return [(part[0], (part[1:7], part[7:13])) + tuple(part[13:]) for part in parts]


def lattice_kernel(f_ref, mask_ref, water_ref, low_ref, high_ref, left_ref, right_ref, clow_ref,
                   chigh_ref, out_ref, *scratch):
    refs = window_refs(scratch)
    layers, height = f_ref.shape[1], f_ref.shape[2]
    lane = lane_index()
    move = 3 * HALO
    left_at = 2 * HALO
    low_tiles = HALO // TILE
    mid_tiles = height // TILE
    half_tiles = mid_tiles // 2
    half_lanes = LANES // 2
    at_end = lane >= LANES - 2 * HALO
    at_left = (lane >= left_at) & (lane < left_at + HALO)
    at_right = lane < HALO

    def join(own, left, right):
        return jnp.where(at_end, own, jnp.where(at_right, right, jnp.where(at_left, left, spin(own, move))))

    for tile in range(2 * low_tiles + mid_tiles):
        if low_tiles <= tile < low_tiles + mid_tiles:
            t = tile - low_tiles
            own_rows = slice(TILE * t, TILE * (t + 1))
            rows = slice(TILE * (t % half_tiles), TILE * (t % half_tiles) + TILE)
            first = half_lanes * (t // half_tiles)

            def own_of(i, z, own_rows=own_rows):
                return f_ref[i, z, own_rows, :] if i < DIRS else mask_ref[z, own_rows, :].astype(jnp.float32)

            def halo(i, z, rows=rows, first=first):
                at = first + HALO * z
                return spin(left_ref[i, rows, :], left_at - at), spin(right_ref[i, rows, :], -at)

            own, extra = (water_ref[k, own_rows, :] for k in range(2))
        else:
            t = tile if tile < low_tiles else tile - low_tiles - mid_tiles
            own_ref, corner_ref = (low_ref, clow_ref) if tile < low_tiles else (high_ref, chigh_ref)
            rows = slice(TILE * t, TILE * (t + 1))

            def own_of(i, z, rows=rows, own_ref=own_ref):
                return own_ref[i, z, rows, :]

            def halo(i, z, rows=rows, corner_ref=corner_ref):
                both = corner_ref[i, rows, :]
                return spin(both, left_at - HALO * z), spin(both, -half_lanes - HALO * z)

            own, extra = (corner_ref[DIRS + 1 + k, rows, :] for k in range(2))

        def edge_of(i, z, own_of=own_of, halo=halo):
            return join(own_of(i, z), *halo(i, z))

        refs[0][5][FRONT + TILE * tile : FRONT + TILE * (tile + 1), :] = own
        refs[1][5][FRONT + TILE * tile : FRONT + TILE * (tile + 1), :] = join(own, spin(extra, move), extra)
        begin(own_of, lambda z, f=own_of: f(DIRS, z), TILE * tile, 0, layers, refs)
        begin(edge_of, lambda z, f=edge_of: f(DIRS, z), TILE * tile, 1, layers, refs)
    first_folds(refs, layers, height + 2 * HALO)
    run_steps(refs, layers, height + 2 * HALO)
    finish(out_ref, refs, layers, height)


def strip_kernel(me_ref, f_ref, mask_ref, ends_ref, left_ref, right_ref, payload_ref):
    layers, height = f_ref.shape[1], f_ref.shape[2]
    lane = lane_index()
    half_rows = height // 2
    half_lanes = LANES // 2

    def pack(i, read):
        for t in range(half_rows // TILE):
            rows = slice(TILE * t, TILE * (t + 1))
            first = last = None
            for h in range(2):
                for z in range(layers):
                    tile = read(z, slice(half_rows * h + TILE * t, half_rows * h + TILE * (t + 1)))
                    at = half_lanes * h + HALO * z
                    one = spin(tile, at)
                    two = spin(tile, at + HALO)
                    mine = lane >= at
                    first = one if first is None else jnp.where(mine, one, first)
                    last = two if last is None else jnp.where(mine, two, last)
            left_ref[i, rows, :] = first
            right_ref[i, rows, :] = last

    for i in range(DIRS):
        pack(i, lambda z, rows, i=i: f_ref[i, z, rows, :])
    pack(DIRS, lambda z, rows: mask_ref[z, rows, :].astype(jnp.float32))

    groups = payload_ref.shape[0]
    peers = groups // 2
    sub = LANES // groups
    tiles = height // TILE
    early = me_ref[0] < peers
    surface = []
    for t in range(tiles):
        rho = f_ref[0, 0, TILE * t : TILE * (t + 1), :]
        for i in range(1, DIRS):
            rho = rho + f_ref[i, 0, TILE * t : TILE * (t + 1), :]
        surface.append(rho)
    for which in range(2):
        ends = [ends_ref[which, TILE * t : TILE * (t + 1), :] for t in range(tiles)]
        for g in range(peers):
            e = which * peers + g
            after, before = (g + 1) % peers, (g + peers - 1) % peers
            water = density = None
            for kind in range(2):
                for t in range(tiles):
                    at = (kind * tiles + t) * sub
                    if kind == 0:
                        piece = spin(ends[t], at - g * sub)
                    else:
                        piece = jnp.where(early, spin(ends[t], at - after * sub), spin(ends[t], at - before * sub))
                    water = piece if water is None else jnp.where(lane >= at, piece, water)
            for t in range(tiles):
                piece = spin(surface[t], (t - e) * sub)
                density = piece if density is None else jnp.where(lane >= t * sub, piece, density)
            payload_ref[e, :TILE, :] = water
            payload_ref[e, TILE:, :] = density


def corner_kernel(got_ref, left_ref, right_ref, up_ref, down_ref, water_ref):
    half_lanes = LANES // 2
    lane = lane_index()
    groups = got_ref.shape[0]
    sub = LANES // groups
    height = water_ref.shape[1]
    tiles = height // TILE
    for kind in range(2):
        for t in range(tiles):
            rows = slice(TILE * t, TILE * (t + 1))
            value = None
            for c in range(groups):
                piece = spin(got_ref[c, :TILE, :], (c - kind * tiles - t) * sub)
                value = piece if value is None else jnp.where(lane >= c * sub, piece, value)
            water_ref[kind, rows, :] = value
            if TILE * t >= height - HALO:
                up_ref[DIRS + 1 + kind, TILE * t - height + HALO : TILE * (t + 1) - height + HALO, :] = value
            if TILE * t < HALO:
                down_ref[DIRS + 1 + kind, rows, :] = value
    for i in range(DIRS + 1):
        for t in range(HALO // TILE):
            rows = slice(TILE * t, TILE * (t + 1))
            left, right = left_ref[i, rows, :], right_ref[i, rows, :]
            up_ref[i, rows, :] = jnp.where(lane < half_lanes, spin(left, half_lanes), right)
            down_ref[i, rows, :] = jnp.where(lane < half_lanes, left, spin(right, half_lanes))


def sheet_kernel(got_ref, sheet_ref, current_ref, out_ref):
    groups = got_ref.shape[0]
    peers = groups // 2
    sub = LANES // groups
    cells, height, columns = sheet_ref.shape
    lane = lane_index()
    for t in range(height // TILE):
        rows = slice(TILE * t, TILE * (t + 1))
        inflow = []
        for which in range(2):
            rho = None
            for g in range(peers):
                piece = spin(got_ref[which * peers + g, TILE:, :], (g - t) * sub)
                rho = piece if rho is None else jnp.where(lane >= g * sub, piece, rho)
            end = sheet_ref[0 if which == 0 else cells - 1, rows, :]
            inflow.append(uptake_rate * (uptake(rho[:, :columns]) - end))
        drag = drag_rate * current_ref[rows, :]
        source = sheet_ref
        for _ in range(SUBSTEPS):
            below = source[0, rows, :]
            spread_below = base_diffusion + slope_diffusion * below
            entering = inflow[0]
            for k in range(cells):
                if k + 1 < cells:
                    above = source[k + 1, rows, :]
                    spread = base_diffusion + slope_diffusion * above
                    leaving = -0.5 * (spread + spread_below) * (above - below) + drag * below
                else:
                    above = spread = None
                    leaving = -inflow[1]
                out_ref[k, rows, :] = below + (entering - leaving)
                below, spread_below, entering = above, spread, leaving
            source = out_ref


def ring(axis, shift):
    count = lax.axis_size(axis)
    return [(i, (i + shift) % count) for i in range(count)]


def on_device(populations, solid_mask, water_sheet, current):
    lattice = populations[0]
    solids = solid_mask[0]
    layers, height, width = lattice.shape[1:]
    groups = lax.axis_size(("side", "gy"))
    f32 = jnp.float32
    mask_values = solids.astype(f32)[None]

    def shape(*dims):
        return jax.ShapeDtypeStruct(dims, f32)

    def rows_of(cut):
        return jnp.concatenate([lattice[:, :, cut], mask_values[:, :, cut]])

    low = lax.ppermute(rows_of(slice(height - HALO, height)), "gx", ring("gx", 1))
    high = lax.ppermute(rows_of(slice(0, HALO)), "gx", ring("gx", -1))

    ends = jnp.stack([water_sheet[0], water_sheet[-1]])
    ends = jnp.pad(ends, ((0, 0), (0, 0), (0, LANES - ends.shape[2])))
    me = lax.axis_index(("side", "gy")).reshape(1)
    strip = shape(DIRS + 1, height // 2, LANES)
    send_left, send_right, payload = pl.pallas_call(
        strip_kernel, out_shape=(strip, strip, shape(groups, 2 * TILE, LANES)),
        in_specs=[pl.BlockSpec(memory_space=pltpu.SMEM), VMEM, VMEM, VMEM], out_specs=(VMEM,) * 3,
        compiler_params=pltpu.CompilerParams(vmem_limit_bytes=8 << 20),
    )(me, lattice, solids, ends)
    left = lax.ppermute(send_right, "gy", ring("gy", 1))
    right = lax.ppermute(send_left, "gy", ring("gy", -1))
    got = lax.all_to_all(payload, ("side", "gy"), split_axis=0, concat_axis=0, tiled=True)

    corner = shape(DIRS + 3, HALO, LANES)
    send_up, send_down, water_here = pl.pallas_call(
        corner_kernel, out_shape=(corner, corner, shape(2, height, width)),
        in_specs=[VMEM] * 3, out_specs=(VMEM,) * 3,
        compiler_params=pltpu.CompilerParams(vmem_limit_bytes=8 << 20),
    )(got, left, right)
    corner_low = lax.ppermute(send_up, "gx", ring("gx", 1))
    corner_high = lax.ppermute(send_down, "gx", ring("gx", -1))
    water = pl.pallas_call(
        sheet_kernel, out_shape=shape(*water_sheet.shape),
        in_specs=[VMEM] * 3, out_specs=VMEM,
        compiler_params=pltpu.CompilerParams(vmem_limit_bytes=8 << 20),
    )(got, water_sheet, current)
    out = pl.pallas_call(
        lattice_kernel, out_shape=shape(*lattice.shape),
        in_specs=[VMEM] * 9, out_specs=VMEM,
        compiler_params=pltpu.CompilerParams(vmem_limit_bytes=36 << 20),
        scratch_shapes=window_scratch(layers, height + 2 * HALO),
        cost_estimate=pl.CostEstimate(flops=1 << 28, bytes_accessed=8 << 20, transcendentals=0),
    )(lattice, solids, water_here, low, high, left, right, corner_low, corner_high)
    return (out[None], water)


def solution(mesh):
    in_specs = (
        P("side", None, None, "gx", "gy"),
        P("side", None, "gx", "gy"),
        P(None, "gx", ("side", "gy")),
        P("gx", ("side", "gy")),
    )
    out_specs = (P("side", None, None, "gx", "gy"), P(None, "gx", ("side", "gy")))
    return jax.shard_map(
        on_device, mesh=mesh, in_specs=in_specs, out_specs=out_specs, check_vma=False
    )
```

```python
import jax
import jax.numpy as jnp
from jax import lax
from jax.experimental import pallas as pl
from jax.experimental.pallas import tpu as pltpu
from jax.sharding import PartitionSpec as P


STEPS = 8
SUBSTEPS = 2
HALO = 2 * STEPS
TILE = 8
FRONT = TILE
LANES = 128
WINDOWS = 2

velocity_table = (
    (0, 0, 0),
    (1, 0, 0),
    (-1, 0, 0),
    (0, 1, 0),
    (0, -1, 0),
    (0, 0, 1),
    (0, 0, -1),
    (1, 1, 0),
    (-1, -1, 0),
    (1, -1, 0),
    (-1, 1, 0),
    (1, 0, 1),
    (-1, 0, -1),
    (1, 0, -1),
    (-1, 0, 1),
    (0, 1, 1),
    (0, -1, -1),
    (0, 1, -1),
    (0, -1, 1),
)
DIRS = len(velocity_table)
wall_potential = 0.4
uptake_rate = 0.02
drag_rate = 0.03
base_diffusion = 0.05
slope_diffusion = 0.015

VMEM = pl.BlockSpec(memory_space=pltpu.VMEM)


def uptake(density_row):
    activity = density_row / (1.0 + density_row)
    return 0.043 + activity * (17.18 + activity * (-39.85 + 36.0 * activity))


def spin(tile, shift):
    shift = shift % LANES
    return tile if shift == 0 else pltpu.roll(tile, shift, 1)


def lane_index():
    return lax.broadcasted_iota(jnp.int32, (TILE, LANES), 1)


def set_pairs(values, row, z, even_ref, odd_ref, rest_ref, density_ref, psi_ref, pore):
    rows = pl.ds(row, TILE)
    if rest_ref is not None:
        rest_ref[z, rows, :] = values[0]
    rho = values[0]
    partial = []
    for k in range(9):
        one, two = values[2 * k + 1], values[2 * k + 2]
        both = one + two
        even_ref[k, z, rows, :] = both
        odd_ref[k, z, rows, :] = one - two
        partial.append(both)
    while len(partial) > 1:
        partial = [a + b for a, b in zip(partial[::2], partial[1::2])] + (
            [partial[-1]] if len(partial) % 2 else []
        )
    rho = rho + partial[0]
    density_ref[z, rows, :] = rho
    psi_ref[z, rows, :] = jnp.where(pore > 0.0, 1.0 - jnp.exp(-rho), wall_potential)
    return rho


def run_steps(refs, layers, window_rows):
    planes = [(0, z, z) for z in range(layers)]

    def across(values, base, z, sign):
        above = values[base + z + 1] if z + 1 < layers else None
        below = values[base + z - 1] if z > 0 else None
        if above is None and below is None:
            return jnp.zeros((TILE, LANES), jnp.float32)
        if above is None:
            return below if sign > 0 else -below
        if below is None:
            return above
        return above + below if sign > 0 else above - below

    def gather(row, window, parity):
        row = row + FRONT
        posts, sets, share_ref = refs[window][:3]
        target = sets[parity]
        even_ref, odd_ref, density_ref, psi_ref = target[:4]
        rows = pl.ds(row, TILE)
        for base, p, z in planes:
            values = []
            for i in range(DIRS):
                _, shift_y, shift_z = velocity_table[i]
                reflected = z - shift_z < 0 or z - shift_z >= layers
                values.append(spin(posts[i, p, rows, :], 0 if reflected else shift_y))
            set_pairs(values, row, p, even_ref, odd_ref, None, density_ref, psi_ref, share_ref[p, rows, :])

    def fold(row, window, parity):
        row = row + FRONT
        _, _, _, psi_ref, around_ref, tilt_ref = refs[window][1][parity]
        rows = pl.ds(row, TILE)
        for base, p, z in planes:
            centre = psi_ref[p, rows, :]
            left, right = spin(centre, 1), spin(centre, -1)
            around_ref[p, rows, :] = (centre + centre) + (left + right)
            tilt_ref[p, rows, :] = right - left

    def collide(row, window, parity):
        row = row + FRONT
        posts, sets, share_ref, even_keep_ref, odd_keep_ref, flux_ref = refs[window]
        even_ref, odd_ref, density_ref, psi_ref, around_ref, tilt_ref = sets[parity]
        rows, up, down = (pl.ds(row + shift, TILE) for shift in (0, 1, -1))
        slope, column, tilt = {}, {}, {}
        for base, p, z in planes:
            for q in range(max(base, p - 1), min(base + layers, p + 2)):
                if q not in slope:
                    plus, minus = psi_ref[q, up, :], psi_ref[q, down, :]
                    slope[q] = plus - minus
                    column[q] = (plus + minus) + around_ref[q, rows, :]
                    tilt[q] = tilt_ref[q, rows, :]
            pulls = (
                (around_ref[p, up, :] - around_ref[p, down, :]) + across(slope, base, z, 1),
                ((tilt[p] + tilt[p]) + (tilt_ref[p, up, :] + tilt_ref[p, down, :]))
                + across(tilt, base, z, 1),
                across(column, base, z, -1),
            )
            rho = density_ref[p, rows, :]
            delta = [None] + [odd_ref[k, p, rows, :] for k in range(9)]
            pulled = psi_ref[p, rows, :] * (1.0 / 15.0)
            a_diag = rho * share_ref[p, rows, :]
            scale = jnp.where(share_ref[p, rows, :] > 0.0, 1.5 / rho, 0.0)
            u = []
            for component in range(3):
                value = None
                for k in range(1, 10):
                    factor = velocity_table[2 * k - 1][component]
                    if factor:
                        if value is None:
                            value = delta[k]
                        else:
                            value = value + delta[k] if factor > 0 else value - delta[k]
                u.append((value + pulled * pulls[component]) * scale)
            b_diag = a_diag - a_diag * ((u[0] * u[0] + u[1] * u[1] + u[2] * u[2]) * (2.0 / 3.0))
            b_axis = b_diag + b_diag
            o_diag = a_diag + a_diag
            o_axis = o_diag + o_diag
            keep_even = even_keep_ref[p, rows, :]
            keep_odd = odd_keep_ref[p, rows, :]
            posts[0, p, rows, :] = posts[0, p, rows, :] * (keep_even + keep_even) + b_diag * 12.0
            for k in range(1, 10):
                i = 2 * k - 1
                e = velocity_table[i]
                along = None
                for component in range(3):
                    if e[component] == 0:
                        continue
                    if along is None:
                        along = u[component]
                    elif e[component] > 0:
                        along = along + u[component]
                    else:
                        along = along - u[component]
                axis = k <= 3
                drift = along * (o_axis if axis else o_diag)
                even = (even_ref[k - 1, p, rows, :] * keep_even + (b_axis if axis else b_diag)) + drift * along
                odd = delta[k] * keep_odd + drift
                for j, sign, post in ((i, 1, even + odd), (i + 1, -1, even - odd)):
                    other = i + 1 if j == i else i
                    shift_x, _, shift_z = (sign * v for v in e)
                    if z + shift_z < 0:
                        inflow = flux_ref[rows, :] * (1.0 / 3.0 if axis else 1.0 / 6.0)
                        posts[other, p, rows, :] = post - inflow
                    elif z + shift_z >= layers:
                        posts[other, p, rows, :] = post
                    else:
                        posts[j, p + shift_z, pl.ds(row + shift_x, TILE), :] = post

    def tiles_of(step):
        return (window_rows - 2 - 4 * step + TILE - 1) // TILE

    for step in range(STEPS):
        half = step % 2
        first = 2 * step + 1
        if step:
            last = 2 * (step - 1) + TILE * (tiles_of(step - 1) - 1)
            for window in range(WINDOWS):
                gather(last, window, half)
            for window in range(WINDOWS):
                collide(first, window, half)
            for window in range(WINDOWS):
                fold(last - TILE, window, half)
            for window in range(WINDOWS):
                fold(last, window, half)
        else:
            for window in range(WINDOWS):
                collide(first, window, half)

        def turn(tile, carry, first=first, half=half):
            row = TILE * tile + first
            gather(row - 1 - TILE, 0, 1 - half)
            gather(row - 1 - TILE, 1, 1 - half)
            collide(row, 0, half)
            collide(row, 1, half)
            fold(row - 1 - 2 * TILE, 0, 1 - half)
            fold(row - 1 - 2 * TILE, 1, 1 - half)
            return carry

        lax.fori_loop(1, tiles_of(step), turn, 0)
    for window in range(WINDOWS):
        gather(2 * (STEPS - 1) + TILE * (tiles_of(STEPS - 1) - 1), window, STEPS % 2)


def first_folds(refs, layers, window_rows):
    for tile in range(window_rows // TILE):
        rows = slice(FRONT + TILE * tile, FRONT + TILE * (tile + 1))
        for window in range(WINDOWS):
            psi_ref, around_ref, tilt_ref = refs[window][1][0][3:6]
            for z in range(layers):
                centre = psi_ref[z, rows, :]
                left, right = spin(centre, 1), spin(centre, -1)
                around_ref[z, rows, :] = (centre + centre) + (left + right)
                tilt_ref[z, rows, :] = right - left


def begin(read, read_pore, row, window, layers, refs):
    posts, sets, share_ref, even_keep_ref, odd_keep_ref, flux_ref = refs[window]
    even_ref, odd_ref, density_ref, psi_ref = sets[0][:4]
    row = row + FRONT
    rows = pl.ds(row, TILE)
    for z in range(layers):
        p = z
        pore = read_pore(z)
        is_pore = pore > 0.5
        share_ref[p, rows, :] = jnp.where(is_pore, 1.25 / 36.0, 0.0)
        even_keep_ref[p, rows, :] = jnp.where(is_pore, -0.125, 0.5)
        odd_keep_ref[p, rows, :] = jnp.where(is_pore, -0.125, -0.5)
        values = [read(i, z) for i in range(DIRS)]
        rho = set_pairs(values, row, p, even_ref, odd_ref, posts.at[0], density_ref, psi_ref, pore)
        if z == 0:
            flux_ref[rows, :] = uptake_rate * (uptake(rho) - flux_ref[rows, :])


def finish(out_ref, refs, layers, height):
    lane = lane_index()
    inside = (lane >= HALO) & (lane < LANES - HALO)
    move = 3 * HALO

    def tile_out(t, carry):
        rows = pl.ds(FRONT + HALO + TILE * t, TILE)
        to = pl.ds(pl.multiple_of(TILE * t, TILE), TILE)

        def join(read):
            middle, edge = read(0), read(1)
            edge = jnp.where(lane < LANES // 2, spin(edge, -move), edge)
            return jnp.where(inside, middle, edge)

        for z in range(layers):
            out_ref[0, z, to, :] = join(lambda w: refs[w][0][0, z, rows, :])
            for k in range(9):
                even = join(lambda w: refs[w][1][STEPS % 2][0][k, z, rows, :]) * 0.5
                odd = join(lambda w: refs[w][1][STEPS % 2][1][k, z, rows, :]) * 0.5
                out_ref[2 * k + 1, z, to, :] = even + odd
                out_ref[2 * k + 2, z, to, :] = even - odd
        return carry

    lax.fori_loop(0, height // TILE, tile_out, 0)


def window_scratch(layers, rows):
    padded = FRONT + rows + 2 * TILE

    def one(*lead):
        return pltpu.VMEM(lead + (padded, LANES), jnp.float32)

    state = [one(9, layers), one(9, layers)] + [one(layers)] * 4
    return ([one(DIRS, layers)] + state + state + [one(layers)] * 3 + [one()]) * WINDOWS


def window_refs(scratch):
    count = len(scratch) // WINDOWS
    parts = [scratch[count * w : count * (w + 1)] for w in range(WINDOWS)]
    return [(part[0], (part[1:7], part[7:13])) + tuple(part[13:]) for part in parts]


def lattice_kernel(f_ref, mask_ref, water_ref, low_ref, high_ref, left_ref, right_ref, clow_ref,
                   chigh_ref, out_ref, *scratch):
    refs = window_refs(scratch)
    layers, height = f_ref.shape[1], f_ref.shape[2]
    lane = lane_index()
    move = 3 * HALO
    left_at = 2 * HALO
    low_tiles = HALO // TILE
    mid_tiles = height // TILE
    half_tiles = mid_tiles // 2
    half_lanes = LANES // 2
    at_end = lane >= LANES - 2 * HALO
    at_left = (lane >= left_at) & (lane < left_at + HALO)
    at_right = lane < HALO

    def join(own, left, right):
        return jnp.where(at_end, own, jnp.where(at_right, right, jnp.where(at_left, left, spin(own, move))))

    for tile in range(2 * low_tiles + mid_tiles):
        if low_tiles <= tile < low_tiles + mid_tiles:
            t = tile - low_tiles
            own_rows = slice(TILE * t, TILE * (t + 1))
            rows = slice(TILE * (t % half_tiles), TILE * (t % half_tiles) + TILE)
            first = half_lanes * (t // half_tiles)

            def own_of(i, z, own_rows=own_rows):
                return f_ref[i, z, own_rows, :] if i < DIRS else mask_ref[z, own_rows, :].astype(jnp.float32)

            def halo(i, z, rows=rows, first=first):
                at = first + HALO * z
                return spin(left_ref[i, rows, :], left_at - at), spin(right_ref[i, rows, :], -at)

            own, extra = (water_ref[k, own_rows, :] for k in range(2))
        else:
            t = tile if tile < low_tiles else tile - low_tiles - mid_tiles
            own_ref, corner_ref = (low_ref, clow_ref) if tile < low_tiles else (high_ref, chigh_ref)
            rows = slice(TILE * t, TILE * (t + 1))

            def own_of(i, z, rows=rows, own_ref=own_ref):
                return own_ref[i, z, rows, :]

            def halo(i, z, rows=rows, corner_ref=corner_ref):
                both = corner_ref[i, rows, :]
                return spin(both, left_at - HALO * z), spin(both, -half_lanes - HALO * z)

            own, extra = (corner_ref[DIRS + 1 + k, rows, :] for k in range(2))

        def edge_of(i, z, own_of=own_of, halo=halo):
            return join(own_of(i, z), *halo(i, z))

        refs[0][5][FRONT + TILE * tile : FRONT + TILE * (tile + 1), :] = own
        refs[1][5][FRONT + TILE * tile : FRONT + TILE * (tile + 1), :] = join(own, spin(extra, move), extra)
        begin(own_of, lambda z, f=own_of: f(DIRS, z), TILE * tile, 0, layers, refs)
        begin(edge_of, lambda z, f=edge_of: f(DIRS, z), TILE * tile, 1, layers, refs)
    first_folds(refs, layers, height + 2 * HALO)
    run_steps(refs, layers, height + 2 * HALO)
    finish(out_ref, refs, layers, height)


def pack_kernel(me_ref, f_hbm, mask_hbm, sheet_hbm, last_ref, first_ref, left_ref, right_ref, payload_ref,
                f_ref, mask_ref, cells_ref, ends_ref, sems):
    layers, height = f_ref.shape[1], f_ref.shape[2]
    lane = lane_index()
    half_rows = height // 2
    half_lanes = LANES // 2
    columns = cells_ref.shape[2]

    load = pltpu.make_async_copy(f_hbm, f_ref, sems.at[0])
    load.start()
    load_mask = pltpu.make_async_copy(mask_hbm, mask_ref, sems.at[1])
    load_mask.start()
    loads = [
        pltpu.make_async_copy(sheet_hbm.at[cell], cells_ref.at[which], sems.at[2 + which])
        for which, cell in enumerate((0, sheet_hbm.shape[0] - 1))
    ]
    for copy in loads:
        copy.start()
    for copy in loads:
        copy.wait()
    ends_ref[...] = jnp.zeros(ends_ref.shape, jnp.float32)
    for which in range(2):
        ends_ref[which, :, :columns] = cells_ref[which]
    load_mask.wait()
    load.wait()

    for i in range(DIRS):
        last_ref[i] = f_ref[i, :, height - HALO :, :]
        first_ref[i] = f_ref[i, :, :HALO, :]
    last_ref[DIRS] = mask_ref[:, height - HALO :, :].astype(jnp.float32)
    first_ref[DIRS] = mask_ref[:, :HALO, :].astype(jnp.float32)

    def pack(i, read):
        for t in range(half_rows // TILE):
            rows = slice(TILE * t, TILE * (t + 1))
            first = last = None
            for h in range(2):
                for z in range(layers):
                    tile = read(z, slice(half_rows * h + TILE * t, half_rows * h + TILE * (t + 1)))
                    at = half_lanes * h + HALO * z
                    one = spin(tile, at)
                    two = spin(tile, at + HALO)
                    mine = lane >= at
                    first = one if first is None else jnp.where(mine, one, first)
                    last = two if last is None else jnp.where(mine, two, last)
            left_ref[i, rows, :] = first
            right_ref[i, rows, :] = last

    for i in range(DIRS):
        pack(i, lambda z, rows, i=i: f_ref[i, z, rows, :])
    pack(DIRS, lambda z, rows: mask_ref[z, rows, :].astype(jnp.float32))

    groups = payload_ref.shape[0]
    peers = groups // 2
    sub = LANES // groups
    tiles = height // TILE
    early = me_ref[0] < peers
    surface = []
    for t in range(tiles):
        rho = f_ref[0, 0, TILE * t : TILE * (t + 1), :]
        for i in range(1, DIRS):
            rho = rho + f_ref[i, 0, TILE * t : TILE * (t + 1), :]
        surface.append(rho)
    for which in range(2):
        ends = [ends_ref[which, TILE * t : TILE * (t + 1), :] for t in range(tiles)]
        for g in range(peers):
            e = which * peers + g
            after, before = (g + 1) % peers, (g + peers - 1) % peers
            water = density = None
            for kind in range(2):
                for t in range(tiles):
                    at = (kind * tiles + t) * sub
                    if kind == 0:
                        piece = spin(ends[t], at - g * sub)
                    else:
                        piece = jnp.where(early, spin(ends[t], at - after * sub), spin(ends[t], at - before * sub))
                    water = piece if water is None else jnp.where(lane >= at, piece, water)
            for t in range(tiles):
                piece = spin(surface[t], (t - e) * sub)
                density = piece if density is None else jnp.where(lane >= t * sub, piece, density)
            payload_ref[e, :TILE, :] = water
            payload_ref[e, TILE:, :] = density


def corner_kernel(got_ref, left_ref, right_ref, up_ref, down_ref, water_ref):
    half_lanes = LANES // 2
    lane = lane_index()
    groups = got_ref.shape[0]
    sub = LANES // groups
    height = water_ref.shape[1]
    tiles = height // TILE
    for kind in range(2):
        for t in range(tiles):
            rows = slice(TILE * t, TILE * (t + 1))
            value = None
            for c in range(groups):
                piece = spin(got_ref[c, :TILE, :], (c - kind * tiles - t) * sub)
                value = piece if value is None else jnp.where(lane >= c * sub, piece, value)
            water_ref[kind, rows, :] = value
            if TILE * t >= height - HALO:
                up_ref[DIRS + 1 + kind, TILE * t - height + HALO : TILE * (t + 1) - height + HALO, :] = value
            if TILE * t < HALO:
                down_ref[DIRS + 1 + kind, rows, :] = value
    for i in range(DIRS + 1):
        for t in range(HALO // TILE):
            rows = slice(TILE * t, TILE * (t + 1))
            left, right = left_ref[i, rows, :], right_ref[i, rows, :]
            up_ref[i, rows, :] = jnp.where(lane < half_lanes, spin(left, half_lanes), right)
            down_ref[i, rows, :] = jnp.where(lane < half_lanes, left, spin(right, half_lanes))


def sheet_kernel(got_ref, sheet_ref, current_ref, out_ref):
    groups = got_ref.shape[0]
    peers = groups // 2
    sub = LANES // groups
    cells, height, columns = sheet_ref.shape
    lane = lane_index()
    for t in range(height // TILE):
        rows = slice(TILE * t, TILE * (t + 1))
        inflow = []
        for which in range(2):
            rho = None
            for g in range(peers):
                piece = spin(got_ref[which * peers + g, TILE:, :], (g - t) * sub)
                rho = piece if rho is None else jnp.where(lane >= g * sub, piece, rho)
            end = sheet_ref[0 if which == 0 else cells - 1, rows, :]
            inflow.append(uptake_rate * (uptake(rho[:, :columns]) - end))
        drag = drag_rate * current_ref[rows, :]
        source = sheet_ref
        for _ in range(SUBSTEPS):
            below = source[0, rows, :]
            spread_below = base_diffusion + slope_diffusion * below
            entering = inflow[0]
            for k in range(cells):
                if k + 1 < cells:
                    above = source[k + 1, rows, :]
                    spread = base_diffusion + slope_diffusion * above
                    leaving = -0.5 * (spread + spread_below) * (above - below) + drag * below
                else:
                    above = spread = None
                    leaving = -inflow[1]
                out_ref[k, rows, :] = below + (entering - leaving)
                below, spread_below, entering = above, spread, leaving
            source = out_ref


def ring(axis, shift):
    count = lax.axis_size(axis)
    return [(i, (i + shift) % count) for i in range(count)]


def on_device(populations, solid_mask, water_sheet, current):
    lattice = populations[0]
    solids = solid_mask[0]
    layers, height, width = lattice.shape[1:]
    groups = lax.axis_size(("side", "gy"))
    f32 = jnp.float32

    def shape(*dims):
        return jax.ShapeDtypeStruct(dims, f32)

    me = lax.axis_index(("side", "gy")).reshape(1)
    strip = shape(DIRS + 1, height // 2, LANES)
    band = shape(DIRS + 1, layers, HALO, width)
    send_last, send_first, send_left, send_right, payload = pl.pallas_call(
        pack_kernel, out_shape=(band, band, strip, strip, shape(groups, 2 * TILE, LANES)),
        in_specs=[pl.BlockSpec(memory_space=pltpu.SMEM)] + [pl.BlockSpec(memory_space=pltpu.HBM)] * 3,
        out_specs=(VMEM,) * 5,
        scratch_shapes=[
            pltpu.VMEM(lattice.shape, f32),
            pltpu.VMEM(solids.shape, jnp.int32),
            pltpu.VMEM((2,) + water_sheet.shape[1:], f32),
            pltpu.VMEM((2, height, width), f32),
            pltpu.SemaphoreType.DMA((4,)),
        ],
        compiler_params=pltpu.CompilerParams(vmem_limit_bytes=62000000),
    )(me, lattice, solids, water_sheet)
    low = lax.ppermute(send_last, "gx", ring("gx", 1))
    high = lax.ppermute(send_first, "gx", ring("gx", -1))
    left = lax.ppermute(send_right, "gy", ring("gy", 1))
    right = lax.ppermute(send_left, "gy", ring("gy", -1))
    got = lax.all_to_all(payload, ("side", "gy"), split_axis=0, concat_axis=0, tiled=True)

    corner = shape(DIRS + 3, HALO, LANES)
    send_up, send_down, water_here = pl.pallas_call(
        corner_kernel, out_shape=(corner, corner, shape(2, height, width)),
        in_specs=[VMEM] * 3, out_specs=(VMEM,) * 3,
        compiler_params=pltpu.CompilerParams(vmem_limit_bytes=8 << 20),
    )(got, left, right)
    corner_low = lax.ppermute(send_up, "gx", ring("gx", 1))
    corner_high = lax.ppermute(send_down, "gx", ring("gx", -1))
    water = pl.pallas_call(
        sheet_kernel, out_shape=shape(*water_sheet.shape),
        in_specs=[VMEM] * 3, out_specs=VMEM,
        compiler_params=pltpu.CompilerParams(vmem_limit_bytes=8 << 20),
    )(got, water_sheet, current)
    out = pl.pallas_call(
        lattice_kernel, out_shape=shape(*lattice.shape),
        in_specs=[VMEM] * 9, out_specs=VMEM,
        compiler_params=pltpu.CompilerParams(vmem_limit_bytes=36 << 20),
        scratch_shapes=window_scratch(layers, height + 2 * HALO),
        cost_estimate=pl.CostEstimate(flops=1 << 28, bytes_accessed=8 << 20, transcendentals=0),
    )(lattice, solids, water_here, low, high, left, right, corner_low, corner_high)
    return (out[None], water)


def solution(mesh):
    in_specs = (
        P("side", None, None, "gx", "gy"),
        P("side", None, "gx", "gy"),
        P(None, "gx", ("side", "gy")),
        P("gx", ("side", "gy")),
    )
    out_specs = (P("side", None, None, "gx", "gy"), P(None, "gx", ("side", "gy")))
    return jax.shard_map(
        on_device, mesh=mesh, in_specs=in_specs, out_specs=out_specs, check_vma=False
    )
```

```python
import jax
import jax.numpy as jnp
from jax import lax
from jax.experimental import pallas as pl
from jax.experimental.pallas import tpu as pltpu
from jax.sharding import PartitionSpec as P


STEPS = 8
SUBSTEPS = 2
HALO = 2 * STEPS
TILE = 8
FRONT = TILE
LANES = 128
WINDOWS = 2

velocity_table = (
    (0, 0, 0),
    (1, 0, 0),
    (-1, 0, 0),
    (0, 1, 0),
    (0, -1, 0),
    (0, 0, 1),
    (0, 0, -1),
    (1, 1, 0),
    (-1, -1, 0),
    (1, -1, 0),
    (-1, 1, 0),
    (1, 0, 1),
    (-1, 0, -1),
    (1, 0, -1),
    (-1, 0, 1),
    (0, 1, 1),
    (0, -1, -1),
    (0, 1, -1),
    (0, -1, 1),
)
DIRS = len(velocity_table)
wall_potential = 0.4
uptake_rate = 0.02
drag_rate = 0.03
base_diffusion = 0.05
slope_diffusion = 0.015

VMEM = pl.BlockSpec(memory_space=pltpu.VMEM)


def uptake(density_row):
    activity = density_row / (1.0 + density_row)
    return 0.043 + activity * (17.18 + activity * (-39.85 + 36.0 * activity))


def spin(tile, shift):
    shift = shift % LANES
    return tile if shift == 0 else pltpu.roll(tile, shift, 1)


def lane_index():
    return lax.broadcasted_iota(jnp.int32, (TILE, LANES), 1)


def set_pairs(values, row, z, even_ref, odd_ref, rest_ref, density_ref, psi_ref, pore):
    rows = pl.ds(row, TILE)
    if rest_ref is not None:
        rest_ref[z, rows, :] = values[0]
    rho = values[0]
    partial = []
    for k in range(9):
        one, two = values[2 * k + 1], values[2 * k + 2]
        both = one + two
        even_ref[k, z, rows, :] = both
        odd_ref[k, z, rows, :] = one - two
        partial.append(both)
    while len(partial) > 1:
        partial = [a + b for a, b in zip(partial[::2], partial[1::2])] + (
            [partial[-1]] if len(partial) % 2 else []
        )
    rho = rho + partial[0]
    density_ref[z, rows, :] = rho
    psi_ref[z, rows, :] = jnp.where(pore > 0.0, 1.0 - jnp.exp(-rho), wall_potential)
    return rho


def run_steps(refs, layers, window_rows):
    planes = [(0, z, z) for z in range(layers)]

    def across(values, base, z, sign):
        above = values[base + z + 1] if z + 1 < layers else None
        below = values[base + z - 1] if z > 0 else None
        if above is None and below is None:
            return jnp.zeros((TILE, LANES), jnp.float32)
        if above is None:
            return below if sign > 0 else -below
        if below is None:
            return above
        return above + below if sign > 0 else above - below

    def gather(row, window, parity):
        row = row + FRONT
        posts, sets, share_ref = refs[window][:3]
        target = sets[parity]
        even_ref, odd_ref, density_ref, psi_ref = target[:4]
        rows = pl.ds(row, TILE)
        for base, p, z in planes:
            values = []
            for i in range(DIRS):
                _, shift_y, shift_z = velocity_table[i]
                reflected = z - shift_z < 0 or z - shift_z >= layers
                values.append(spin(posts[i, p, rows, :], 0 if reflected else shift_y))
            set_pairs(values, row, p, even_ref, odd_ref, None, density_ref, psi_ref, share_ref[p, rows, :])

    def fold(row, window, parity):
        row = row + FRONT
        _, _, _, psi_ref, around_ref, tilt_ref = refs[window][1][parity]
        rows = pl.ds(row, TILE)
        for base, p, z in planes:
            centre = psi_ref[p, rows, :]
            left, right = spin(centre, 1), spin(centre, -1)
            around_ref[p, rows, :] = (centre + centre) + (left + right)
            tilt_ref[p, rows, :] = right - left

    def collide(row, window, parity):
        row = row + FRONT
        posts, sets, share_ref, even_keep_ref, odd_keep_ref, flux_ref = refs[window]
        even_ref, odd_ref, density_ref, psi_ref, around_ref, tilt_ref = sets[parity]
        rows, up, down = (pl.ds(row + shift, TILE) for shift in (0, 1, -1))
        slope, column, tilt = {}, {}, {}
        for base, p, z in planes:
            for q in range(max(base, p - 1), min(base + layers, p + 2)):
                if q not in slope:
                    plus, minus = psi_ref[q, up, :], psi_ref[q, down, :]
                    slope[q] = plus - minus
                    column[q] = (plus + minus) + around_ref[q, rows, :]
                    tilt[q] = tilt_ref[q, rows, :]
            pulls = (
                (around_ref[p, up, :] - around_ref[p, down, :]) + across(slope, base, z, 1),
                ((tilt[p] + tilt[p]) + (tilt_ref[p, up, :] + tilt_ref[p, down, :]))
                + across(tilt, base, z, 1),
                across(column, base, z, -1),
            )
            rho = density_ref[p, rows, :]
            delta = [None] + [odd_ref[k, p, rows, :] for k in range(9)]
            pulled = psi_ref[p, rows, :] * (1.0 / 15.0)
            a_diag = rho * share_ref[p, rows, :]
            scale = jnp.where(share_ref[p, rows, :] > 0.0, 1.5 / rho, 0.0)
            u = []
            for component in range(3):
                value = None
                for k in range(1, 10):
                    factor = velocity_table[2 * k - 1][component]
                    if factor:
                        if value is None:
                            value = delta[k]
                        else:
                            value = value + delta[k] if factor > 0 else value - delta[k]
                u.append((value + pulled * pulls[component]) * scale)
            b_diag = a_diag - a_diag * ((u[0] * u[0] + u[1] * u[1] + u[2] * u[2]) * (2.0 / 3.0))
            b_axis = b_diag + b_diag
            o_diag = a_diag + a_diag
            o_axis = o_diag + o_diag
            keep_even = even_keep_ref[p, rows, :]
            keep_odd = odd_keep_ref[p, rows, :]
            posts[0, p, rows, :] = posts[0, p, rows, :] * (keep_even + keep_even) + b_diag * 12.0
            for k in range(1, 10):
                i = 2 * k - 1
                e = velocity_table[i]
                along = None
                for component in range(3):
                    if e[component] == 0:
                        continue
                    if along is None:
                        along = u[component]
                    elif e[component] > 0:
                        along = along + u[component]
                    else:
                        along = along - u[component]
                axis = k <= 3
                drift = along * (o_axis if axis else o_diag)
                even = (even_ref[k - 1, p, rows, :] * keep_even + (b_axis if axis else b_diag)) + drift * along
                odd = delta[k] * keep_odd + drift
                for j, sign, post in ((i, 1, even + odd), (i + 1, -1, even - odd)):
                    other = i + 1 if j == i else i
                    shift_x, _, shift_z = (sign * v for v in e)
                    if z + shift_z < 0:
                        inflow = flux_ref[rows, :] * (1.0 / 3.0 if axis else 1.0 / 6.0)
                        posts[other, p, rows, :] = post - inflow
                    elif z + shift_z >= layers:
                        posts[other, p, rows, :] = post
                    else:
                        posts[j, p + shift_z, pl.ds(row + shift_x, TILE), :] = post

    def tiles_of(step):
        return (window_rows - 2 - 4 * step + TILE - 1) // TILE

    for step in range(STEPS):
        half = step % 2
        first = 2 * step + 1
        if step:
            last = 2 * (step - 1) + TILE * (tiles_of(step - 1) - 1)
            for window in range(WINDOWS):
                gather(last, window, half)
            for window in range(WINDOWS):
                collide(first, window, half)
            for window in range(WINDOWS):
                fold(last - TILE, window, half)
            for window in range(WINDOWS):
                fold(last, window, half)
        else:
            for window in range(WINDOWS):
                collide(first, window, half)

        def turn(tile, carry, first=first, half=half):
            row = TILE * tile + first
            gather(row - 1 - TILE, 0, 1 - half)
            gather(row - 1 - TILE, 1, 1 - half)
            collide(row, 0, half)
            collide(row, 1, half)
            fold(row - 1 - 2 * TILE, 0, 1 - half)
            fold(row - 1 - 2 * TILE, 1, 1 - half)
            return carry

        lax.fori_loop(1, tiles_of(step), turn, 0)
    for window in range(WINDOWS):
        gather(2 * (STEPS - 1) + TILE * (tiles_of(STEPS - 1) - 1), window, STEPS % 2)


def first_folds(refs, layers, window_rows):
    for tile in range(window_rows // TILE):
        rows = slice(FRONT + TILE * tile, FRONT + TILE * (tile + 1))
        for window in range(WINDOWS):
            psi_ref, around_ref, tilt_ref = refs[window][1][0][3:6]
            for z in range(layers):
                centre = psi_ref[z, rows, :]
                left, right = spin(centre, 1), spin(centre, -1)
                around_ref[z, rows, :] = (centre + centre) + (left + right)
                tilt_ref[z, rows, :] = right - left


def begin(read, read_pore, row, window, layers, refs):
    posts, sets, share_ref, even_keep_ref, odd_keep_ref, flux_ref = refs[window]
    even_ref, odd_ref, density_ref, psi_ref = sets[0][:4]
    row = row + FRONT
    rows = pl.ds(row, TILE)
    for z in range(layers):
        p = z
        pore = read_pore(z)
        is_pore = pore > 0.5
        share_ref[p, rows, :] = jnp.where(is_pore, 1.25 / 36.0, 0.0)
        even_keep_ref[p, rows, :] = jnp.where(is_pore, -0.125, 0.5)
        odd_keep_ref[p, rows, :] = jnp.where(is_pore, -0.125, -0.5)
        values = [read(i, z) for i in range(DIRS)]
        rho = set_pairs(values, row, p, even_ref, odd_ref, posts.at[0], density_ref, psi_ref, pore)
        if z == 0:
            flux_ref[rows, :] = uptake_rate * (uptake(rho) - flux_ref[rows, :])


def finish(out_ref, refs, layers, height):
    lane = lane_index()
    inside = (lane >= HALO) & (lane < LANES - HALO)
    move = 3 * HALO

    def tile_out(t, carry):
        rows = pl.ds(FRONT + HALO + TILE * t, TILE)
        to = pl.ds(pl.multiple_of(TILE * t, TILE), TILE)

        def join(read):
            middle, edge = read(0), read(1)
            edge = jnp.where(lane < LANES // 2, spin(edge, -move), edge)
            return jnp.where(inside, middle, edge)

        for z in range(layers):
            out_ref[0, z, to, :] = join(lambda w: refs[w][0][0, z, rows, :])
            for k in range(9):
                even = join(lambda w: refs[w][1][STEPS % 2][0][k, z, rows, :]) * 0.5
                odd = join(lambda w: refs[w][1][STEPS % 2][1][k, z, rows, :]) * 0.5
                out_ref[2 * k + 1, z, to, :] = even + odd
                out_ref[2 * k + 2, z, to, :] = even - odd
        return carry

    lax.fori_loop(0, height // TILE, tile_out, 0, unroll=2)


def window_scratch(layers, rows):
    padded = FRONT + rows + 2 * TILE

    def one(*lead):
        return pltpu.VMEM(lead + (padded, LANES), jnp.float32)

    state = [one(9, layers), one(9, layers)] + [one(layers)] * 4
    return ([one(DIRS, layers)] + state + state + [one(layers)] * 3 + [one()]) * WINDOWS


def window_refs(scratch):
    count = len(scratch) // WINDOWS
    parts = [scratch[count * w : count * (w + 1)] for w in range(WINDOWS)]
    return [(part[0], (part[1:7], part[7:13])) + tuple(part[13:]) for part in parts]


def edges_kernel(f_ref, mask_ref, low_ref, high_ref, left_ref, right_ref, out_ref):
    layers, height = f_ref.shape[1], f_ref.shape[2]
    lane = lane_index()
    move = 3 * HALO
    left_at = 2 * HALO
    half_tiles = height // TILE // 2
    at_end = lane >= LANES - 2 * HALO
    at_left = (lane >= left_at) & (lane < left_at + HALO)
    at_right = lane < HALO

    def own(tile):
        return jnp.where(at_end, tile, spin(tile, move))

    for i in range(DIRS + 1):
        for z in range(layers):
            for t in range(HALO // TILE):
                rows = slice(TILE * t, TILE * (t + 1))
                out_ref[i, z, rows, :] = own(low_ref[i, z, rows, :])
                after = slice(HALO + height + TILE * t, HALO + height + TILE * (t + 1))
                out_ref[i, z, after, :] = own(high_ref[i, z, rows, :])
            for t in range(height // TILE):
                own_rows = slice(TILE * t, TILE * (t + 1))
                rows = slice(TILE * (t % half_tiles), TILE * (t % half_tiles) + TILE)
                at = LANES // 2 * (t // half_tiles) + HALO * z
                tile = f_ref[i, z, own_rows, :] if i < DIRS else mask_ref[z, own_rows, :].astype(jnp.float32)
                right = spin(right_ref[i, rows, :], -at)
                left = spin(left_ref[i, rows, :], left_at - at)
                out_ref[i, z, HALO + TILE * t : HALO + TILE * (t + 1), :] = jnp.where(
                    at_right, right, jnp.where(at_left, left, own(tile))
                )


def lattice_kernel(f_ref, mask_ref, water_ref, low_ref, high_ref, edges_ref, clow_ref,
                   chigh_ref, out_ref, *scratch):
    refs = window_refs(scratch)
    layers, height = f_ref.shape[1], f_ref.shape[2]
    lane = lane_index()
    move = 3 * HALO
    left_at = 2 * HALO
    low_tiles = HALO // TILE
    mid_tiles = height // TILE
    half_lanes = LANES // 2
    at_end = lane >= LANES - 2 * HALO
    at_left = (lane >= left_at) & (lane < left_at + HALO)
    at_right = lane < HALO

    for tile in range(2 * low_tiles + mid_tiles):
        window_rows = slice(TILE * tile, TILE * (tile + 1))
        if low_tiles <= tile < low_tiles + mid_tiles:
            t = tile - low_tiles
            own_rows = slice(TILE * t, TILE * (t + 1))

            def own_of(i, z, own_rows=own_rows):
                return f_ref[i, z, own_rows, :] if i < DIRS else mask_ref[z, own_rows, :].astype(jnp.float32)

            def edge_of(i, z, window_rows=window_rows):
                return edges_ref[i, z, window_rows, :]

            own, extra = (water_ref[k, own_rows, :] for k in range(2))
        else:
            t = tile if tile < low_tiles else tile - low_tiles - mid_tiles
            own_ref, corner_ref = (low_ref, clow_ref) if tile < low_tiles else (high_ref, chigh_ref)
            rows = slice(TILE * t, TILE * (t + 1))

            def own_of(i, z, rows=rows, own_ref=own_ref):
                return own_ref[i, z, rows, :]

            def edge_of(i, z, rows=rows, corner_ref=corner_ref, window_rows=window_rows):
                both = corner_ref[i, rows, :]
                left, right = spin(both, left_at - HALO * z), spin(both, -half_lanes - HALO * z)
                return jnp.where(at_right, right, jnp.where(at_left, left, edges_ref[i, z, window_rows, :]))

            own, extra = (corner_ref[DIRS + 1 + k, rows, :] for k in range(2))

        framed = slice(FRONT + TILE * tile, FRONT + TILE * (tile + 1))
        refs[0][5][framed, :] = own
        refs[1][5][framed, :] = jnp.where(
            at_end, own, jnp.where(at_right, extra, jnp.where(at_left, spin(extra, move), spin(own, move)))
        )
        begin(own_of, lambda z, f=own_of: f(DIRS, z), TILE * tile, 0, layers, refs)
        begin(edge_of, lambda z, f=edge_of: f(DIRS, z), TILE * tile, 1, layers, refs)
    first_folds(refs, layers, height + 2 * HALO)
    run_steps(refs, layers, height + 2 * HALO)
    finish(out_ref, refs, layers, height)


def pack_kernel(me_ref, f_hbm, mask_hbm, sheet_hbm, last_ref, first_ref, left_ref, right_ref, payload_ref,
                f_ref, mask_ref, cells_ref, ends_ref, sems):
    layers, height = f_ref.shape[1], f_ref.shape[2]
    lane = lane_index()
    half_rows = height // 2
    half_lanes = LANES // 2
    columns = cells_ref.shape[2]

    load = pltpu.make_async_copy(f_hbm, f_ref, sems.at[0])
    load.start()
    load_mask = pltpu.make_async_copy(mask_hbm, mask_ref, sems.at[1])
    load_mask.start()
    loads = [
        pltpu.make_async_copy(sheet_hbm.at[cell], cells_ref.at[which], sems.at[2 + which])
        for which, cell in enumerate((0, sheet_hbm.shape[0] - 1))
    ]
    for copy in loads:
        copy.start()
    for copy in loads:
        copy.wait()
    ends_ref[...] = jnp.zeros(ends_ref.shape, jnp.float32)
    for which in range(2):
        ends_ref[which, :, :columns] = cells_ref[which]
    load_mask.wait()
    load.wait()

    for i in range(DIRS):
        last_ref[i] = f_ref[i, :, height - HALO :, :]
        first_ref[i] = f_ref[i, :, :HALO, :]
    last_ref[DIRS] = mask_ref[:, height - HALO :, :].astype(jnp.float32)
    first_ref[DIRS] = mask_ref[:, :HALO, :].astype(jnp.float32)

    def pack(i, read):
        for t in range(half_rows // TILE):
            rows = slice(TILE * t, TILE * (t + 1))
            first = last = None
            for h in range(2):
                for z in range(layers):
                    tile = read(z, slice(half_rows * h + TILE * t, half_rows * h + TILE * (t + 1)))
                    at = half_lanes * h + HALO * z
                    one = spin(tile, at)
                    two = spin(tile, at + HALO)
                    mine = lane >= at
                    first = one if first is None else jnp.where(mine, one, first)
                    last = two if last is None else jnp.where(mine, two, last)
            left_ref[i, rows, :] = first
            right_ref[i, rows, :] = last

    for i in range(DIRS):
        pack(i, lambda z, rows, i=i: f_ref[i, z, rows, :])
    pack(DIRS, lambda z, rows: mask_ref[z, rows, :].astype(jnp.float32))

    groups = payload_ref.shape[0]
    peers = groups // 2
    sub = LANES // groups
    tiles = height // TILE
    early = me_ref[0] < peers
    surface = []
    for t in range(tiles):
        rho = f_ref[0, 0, TILE * t : TILE * (t + 1), :]
        for i in range(1, DIRS):
            rho = rho + f_ref[i, 0, TILE * t : TILE * (t + 1), :]
        surface.append(rho)
    for which in range(2):
        ends = [ends_ref[which, TILE * t : TILE * (t + 1), :] for t in range(tiles)]
        for g in range(peers):
            e = which * peers + g
            after, before = (g + 1) % peers, (g + peers - 1) % peers
            water = density = None
            for kind in range(2):
                for t in range(tiles):
                    at = (kind * tiles + t) * sub
                    if kind == 0:
                        piece = spin(ends[t], at - g * sub)
                    else:
                        piece = jnp.where(early, spin(ends[t], at - after * sub), spin(ends[t], at - before * sub))
                    water = piece if water is None else jnp.where(lane >= at, piece, water)
            for t in range(tiles):
                piece = spin(surface[t], (t - e) * sub)
                density = piece if density is None else jnp.where(lane >= t * sub, piece, density)
            payload_ref[e, :TILE, :] = water
            payload_ref[e, TILE:, :] = density


def corner_kernel(got_ref, left_ref, right_ref, up_ref, down_ref, water_ref):
    half_lanes = LANES // 2
    lane = lane_index()
    groups = got_ref.shape[0]
    sub = LANES // groups
    height = water_ref.shape[1]
    tiles = height // TILE
    for kind in range(2):
        for t in range(tiles):
            rows = slice(TILE * t, TILE * (t + 1))
            value = None
            for c in range(groups):
                piece = spin(got_ref[c, :TILE, :], (c - kind * tiles - t) * sub)
                value = piece if value is None else jnp.where(lane >= c * sub, piece, value)
            water_ref[kind, rows, :] = value
            if TILE * t >= height - HALO:
                up_ref[DIRS + 1 + kind, TILE * t - height + HALO : TILE * (t + 1) - height + HALO, :] = value
            if TILE * t < HALO:
                down_ref[DIRS + 1 + kind, rows, :] = value
    for i in range(DIRS + 1):
        for t in range(HALO // TILE):
            rows = slice(TILE * t, TILE * (t + 1))
            left, right = left_ref[i, rows, :], right_ref[i, rows, :]
            up_ref[i, rows, :] = jnp.where(lane < half_lanes, spin(left, half_lanes), right)
            down_ref[i, rows, :] = jnp.where(lane < half_lanes, left, spin(right, half_lanes))


def sheet_kernel(got_ref, sheet_ref, current_ref, out_ref):
    groups = got_ref.shape[0]
    peers = groups // 2
    sub = LANES // groups
    cells, height, columns = sheet_ref.shape
    lane = lane_index()
    for t in range(height // TILE):
        rows = slice(TILE * t, TILE * (t + 1))
        inflow = []
        for which in range(2):
            rho = None
            for g in range(peers):
                piece = spin(got_ref[which * peers + g, TILE:, :], (g - t) * sub)
                rho = piece if rho is None else jnp.where(lane >= g * sub, piece, rho)
            end = sheet_ref[0 if which == 0 else cells - 1, rows, :]
            inflow.append(uptake_rate * (uptake(rho[:, :columns]) - end))
        drag = drag_rate * current_ref[rows, :]
        source = sheet_ref
        for _ in range(SUBSTEPS):
            below = source[0, rows, :]
            spread_below = base_diffusion + slope_diffusion * below
            entering = inflow[0]
            for k in range(cells):
                if k + 1 < cells:
                    above = source[k + 1, rows, :]
                    spread = base_diffusion + slope_diffusion * above
                    leaving = -0.5 * (spread + spread_below) * (above - below) + drag * below
                else:
                    above = spread = None
                    leaving = -inflow[1]
                out_ref[k, rows, :] = below + (entering - leaving)
                below, spread_below, entering = above, spread, leaving
            source = out_ref


def ring(axis, shift):
    count = lax.axis_size(axis)
    return [(i, (i + shift) % count) for i in range(count)]


def on_device(populations, solid_mask, water_sheet, current):
    lattice = populations[0]
    solids = solid_mask[0]
    layers, height, width = lattice.shape[1:]
    groups = lax.axis_size(("side", "gy"))
    f32 = jnp.float32

    def shape(*dims):
        return jax.ShapeDtypeStruct(dims, f32)

    me = lax.axis_index(("side", "gy")).reshape(1)
    strip = shape(DIRS + 1, height // 2, LANES)
    band = shape(DIRS + 1, layers, HALO, width)
    send_last, send_first, send_left, send_right, payload = pl.pallas_call(
        pack_kernel, out_shape=(band, band, strip, strip, shape(groups, 2 * TILE, LANES)),
        in_specs=[pl.BlockSpec(memory_space=pltpu.SMEM)] + [pl.BlockSpec(memory_space=pltpu.HBM)] * 3,
        out_specs=(VMEM,) * 5,
        scratch_shapes=[
            pltpu.VMEM(lattice.shape, f32),
            pltpu.VMEM(solids.shape, jnp.int32),
            pltpu.VMEM((2,) + water_sheet.shape[1:], f32),
            pltpu.VMEM((2, height, width), f32),
            pltpu.SemaphoreType.DMA((4,)),
        ],
        compiler_params=pltpu.CompilerParams(vmem_limit_bytes=62000000),
    )(me, lattice, solids, water_sheet)
    low = lax.ppermute(send_last, "gx", ring("gx", 1))
    high = lax.ppermute(send_first, "gx", ring("gx", -1))
    left = lax.ppermute(send_right, "gy", ring("gy", 1))
    right = lax.ppermute(send_left, "gy", ring("gy", -1))
    got = lax.all_to_all(payload, ("side", "gy"), split_axis=0, concat_axis=0, tiled=True)

    corner = shape(DIRS + 3, HALO, LANES)
    send_up, send_down, water_here = pl.pallas_call(
        corner_kernel, out_shape=(corner, corner, shape(2, height, width)),
        in_specs=[VMEM] * 3, out_specs=(VMEM,) * 3,
        compiler_params=pltpu.CompilerParams(vmem_limit_bytes=8 << 20),
    )(got, left, right)
    corner_low = lax.ppermute(send_up, "gx", ring("gx", 1))
    corner_high = lax.ppermute(send_down, "gx", ring("gx", -1))
    water = pl.pallas_call(
        sheet_kernel, out_shape=shape(*water_sheet.shape),
        in_specs=[VMEM] * 3, out_specs=VMEM,
        compiler_params=pltpu.CompilerParams(vmem_limit_bytes=8 << 20),
    )(got, water_sheet, current)
    edges = pl.pallas_call(
        edges_kernel, out_shape=shape(DIRS + 1, layers, height + 2 * HALO, LANES),
        in_specs=[VMEM] * 6, out_specs=VMEM,
        compiler_params=pltpu.CompilerParams(vmem_limit_bytes=8 << 20),
    )(lattice, solids, low, high, left, right)
    out = pl.pallas_call(
        lattice_kernel, out_shape=shape(*lattice.shape),
        in_specs=[VMEM] * 8, out_specs=VMEM,
        compiler_params=pltpu.CompilerParams(vmem_limit_bytes=36 << 20),
        scratch_shapes=window_scratch(layers, height + 2 * HALO),
        cost_estimate=pl.CostEstimate(flops=1 << 28, bytes_accessed=8 << 20, transcendentals=0),
    )(lattice, solids, water_here, low, high, edges, corner_low, corner_high)
    return (out[None], water)


def solution(mesh):
    in_specs = (
        P("side", None, None, "gx", "gy"),
        P("side", None, "gx", "gy"),
        P(None, "gx", ("side", "gy")),
        P("gx", ("side", "gy")),
    )
    out_specs = (P("side", None, None, "gx", "gy"), P(None, "gx", ("side", "gy")))
    return jax.shard_map(
        on_device, mesh=mesh, in_specs=in_specs, out_specs=out_specs, check_vma=False
    )
```
